256 devices in a mesh: rows: 32 (over y, x, core), cols: 8 (over z).
Axes of the slice: x: 4, y: 4, z: 8, core: 2. Of those that a mesh axis runs over, the one named last changes fastest.
Arguments:
- tiles: float32 [32, 64, 128, 128], P('rows', 'cols'), may hold values from -0.1875 to 0.1875
- tile_rows: int32 [32, 64], P('rows', 'cols'), may hold values from 0 to 1
- tile_cols: int32 [32, 64], P('rows', 'cols'), may hold values from 0 to 15
- counts: int32 [32, 8], P('rows', 'cols'), may hold values from 1 to 8, as said below
- scaling: float32 [16384], P('cols'), may hold values from 0.1 to 10
Outputs:
- normal: float32 [8192, 8192], P('rows', 'cols')
The draws below stay inside these ranges and needn't reach their ends.
Inputs may be any that keep to these rules, and one draw needn't show every extreme that they name: `counts`: in every draw some panels have all 8 slots live in every column group; the others have at most 5.
All inputs are finite; a program needn't handle non-finite values.
Results may differ from the reference program's by a relative error of at most 0.0003.
Values sent between devices are 32-bit elements; how exact they have to be, the bound alone decides.
A program may use at most 192 MiB of HBM per device.

```python
import math
import jax
import jax.numpy as jnp
from jax import lax

TB = 128
RB = 2
CB_DEV = 16
KT = 8
PANELS = 32
GROUPS = 8
NCON = 8192
NVAR = 16384


def draw_counts(key, part):
    first_key, second_key, third_key = jax.random.split(key, 3)
    base_counts = jax.random.randint(first_key, (PANELS, GROUPS), 1, KT // 2 + 2)
    linking = jax.random.randint(second_key, (PANELS,), 0, 8) == 0
    forced = jax.random.randint(third_key, (), 0, PANELS)
    linking = linking | (jnp.arange(PANELS) == forced)
    return jnp.where(linking[:, None], KT, base_counts).astype(jnp.int32)


def plant(array, own_key, low, high):
    longest = array.shape.index(max(array.shape))
    spots = []
    for shift in (0, 1):
        where = [jax.random.randint(jax.random.fold_in(own_key, axis), (), 0, length) for axis, length in enumerate(array.shape)]
        where[longest] = (where[longest] + shift) % array.shape[longest]
        spots.append(tuple(where))
    return array.at[spots[0]].set(low).at[spots[1]].set(high)


def block_levels(stream_key, dims, pieces, smallest, top_value):
    def one(position, shards_of):
        steps = jax.random.uniform(jax.random.fold_in(jax.random.fold_in(stream_key, 6), position), (shards_of,), jnp.float32, smallest / len(pieces), top_value / len(pieces))
        return jnp.repeat(jnp.exp(steps), dims[position] // shards_of).reshape((-1,) + (1,) * (len(dims) - position - 1))

    loudness = one(*pieces[0])
    for cut in pieces[1:]:
        loudness = loudness * one(*cut)
    return loudness


def normal_values(rng, extent, scale, limit, shards=(), kind=jnp.bfloat16):
    drawn = jax.random.normal(rng, extent, jnp.float32) * scale
    if len(shards) > 0:
        drawn = block_levels(rng, extent, shards, -0.22, 0.18) * drawn
    return jnp.clip(drawn, min=-limit, max=limit).astype(kind)


def setup_inputs(seed: int = 0) -> dict:
    keys = jax.random.split(jax.random.key(seed), 6)
    return {
        "tiles": normal_values(keys[0], (PANELS, GROUPS * KT, TB, TB), (TB * KT) ** -0.5, 0.1875, ((0, 32), (1, 8)), jnp.float32),
        "tile_rows": plant(jax.random.randint(keys[1], (PANELS, GROUPS * KT), 0, RB), jax.random.fold_in(keys[1], 1), 0, RB - 1).astype(jnp.int32),
        "tile_cols": plant(jax.random.randint(keys[2], (PANELS, GROUPS * KT), 0, CB_DEV), jax.random.fold_in(keys[2], 1), 0, CB_DEV - 1).astype(jnp.int32),
        "counts": draw_counts(jax.random.fold_in(keys[5], 71), 0),
        "scaling": jnp.clip(jnp.exp(math.log(10.0) - 4.6051702 * jax.random.uniform(keys[4], (NVAR,), jnp.float32) ** block_levels(keys[4], (NVAR,), ((0, 8),), -0.2, 0.2)), 0.1, 10.0),
    }


def densify(tile_set, row_ids, col_ids, live_mask, scale_set):
    hit_col = (col_ids[:, None] == jnp.arange(CB_DEV, dtype=jnp.int32)[None, :]).astype(jnp.float32) * live_mask[:, None]
    hit_row = (row_ids[:, None] == jnp.arange(RB, dtype=jnp.int32)[None, :]).astype(jnp.float32)
    placed = jnp.einsum('kj,kr,kab->jrab', hit_col, hit_row, tile_set, precision=lax.Precision.HIGHEST)
    placed = placed * scale_set[:, None, None, :]
    return placed.reshape(CB_DEV, RB * TB, TB)


def reference(tiles, tile_rows, tile_cols, counts, scaling):
    def group_term(running, group):
        group_tiles = lax.dynamic_slice_in_dim(tiles, group * KT, KT, 1)
        group_rows = lax.dynamic_slice_in_dim(tile_rows, group * KT, KT, 1)
        group_cols = lax.dynamic_slice_in_dim(tile_cols, group * KT, KT, 1)
        group_count = lax.dynamic_slice_in_dim(counts, group, 1, 1)[:, 0]
        group_scale = lax.dynamic_slice_in_dim(scaling, group * CB_DEV * TB, CB_DEV * TB).reshape(CB_DEV, TB)
        live_mask = (jnp.arange(KT, dtype=jnp.int32)[None, :] < group_count[:, None]).astype(jnp.float32)
        blocked = jax.vmap(densify, in_axes=(0, 0, 0, 0, None))(group_tiles, group_rows, group_cols, live_mask, group_scale)

        def column_panel(inputs):
            far_tiles, far_rows, far_cols, far_live = inputs
            picked = jnp.take(blocked, far_cols, axis=1)
            product = jnp.einsum('pkac,kbc->pkab', picked, far_tiles, precision=lax.Precision.HIGHEST)
            hit_row = (far_rows[:, None] == jnp.arange(RB, dtype=jnp.int32)[None, :]).astype(jnp.float32) * far_live[:, None]
            placed = jnp.einsum('kr,pkab->parb', hit_row, product, precision=lax.Precision.HIGHEST)
            return placed.reshape(PANELS, RB * TB, RB * TB)

        columns = lax.map(column_panel, (group_tiles, group_rows, group_cols, live_mask))
        term = jnp.transpose(columns, (1, 2, 0, 3)).reshape(NCON, NCON)
        return running + term, None

    start = jnp.zeros((NCON, NCON), jnp.float32)
    normal, _ = lax.scan(group_term, start, jnp.arange(GROUPS, dtype=jnp.int32))
    return normal
```

```python
import functools

import jax
import jax.numpy as jnp
from jax import lax
from jax.experimental import pallas as pl
from jax.experimental.pallas import tpu as pltpu
from jax.sharding import PartitionSpec as P

TB = 128
RB = 2
CB_DEV = 16
META = 8


def pack(tiles, tile_rows, tile_cols, counts):
    slots = tiles.shape[1]
    meta = jnp.stack(
        [tile_rows[0], tile_cols[0], jnp.broadcast_to(counts[0, 0], (slots,))]
    ).astype(jnp.float32)
    meta = jnp.pad(meta, ((0, META - 3), (0, TB - slots)))
    return jnp.concatenate([tiles[0].reshape(slots * TB, TB), meta], axis=0)


def unpack_meta(sets, slots):
    return sets[:, slots * TB : slots * TB + 3, :slots].astype(jnp.int32).reshape(-1)


def split(x):
    hi = x.astype(jnp.bfloat16)
    lo = (x - hi.astype(jnp.float32)).astype(jnp.bfloat16)
    return hi, lo


def dot_t(a, b):
    return lax.dot_general(a, b, (((1,), (1,)), ((), ())), preferred_element_type=jnp.float32)


def normal_kernel(slots, far_per, own_meta, far_meta, own_ref, far_ref, scal_ref, out_ref, dense, p_hi, p_lo):
    g = pl.program_id(0)

    @pl.when(g == 0)
    def _():
        out_ref[...] = jnp.zeros_like(out_ref)

    dense[...] = jnp.zeros_like(dense)
    own_count = own_meta[(g * 3 + 2) * slots]
    for k in range(slots):

        @pl.when(k < own_count)
        def _():
            r = own_meta[(g * 3 + 0) * slots + k]
            c = own_meta[(g * 3 + 1) * slots + k]
            rows = pl.ds(pl.multiple_of(r * TB, TB), TB)
            cols = pl.ds(pl.multiple_of(c * TB, TB), TB)
            tile = own_ref[0, k * TB : (k + 1) * TB, :]
            dense[rows, cols] += tile * scal_ref[0, pl.ds(c, 1), :]

    hi, lo = split(dense[...])
    p_hi[...] = hi
    p_lo[...] = lo

    def body(t, carry):
        qi = t // slots
        k = t % slots
        base = (g * far_per + qi) * 3 * slots
        count = far_meta[base + 2 * slots]

        @pl.when(k < count)
        def _():
            r = far_meta[base + k]
            c = far_meta[base + slots + k]
            cols = pl.ds(pl.multiple_of(c * TB, TB), TB)
            tile = far_ref[qi, pl.ds(pl.multiple_of(k * TB, TB), TB), :]
            t_hi, t_lo = split(tile)
            a_hi = p_hi[:, cols]
            a_lo = p_lo[:, cols]
            prod = dot_t(a_hi, t_hi) + (dot_t(a_hi, t_lo) + dot_t(a_lo, t_hi))
            dest = pl.ds(pl.multiple_of(qi * RB * TB + r * TB, TB), TB)
            out_ref[:, dest] += prod

        return carry

    lax.fori_loop(0, far_per * slots, body, 0)


def per_device(tiles, tile_rows, tile_cols, counts, scaling):
    n_rows = lax.axis_size("rows")
    n_cols = lax.axis_size("cols")
    slots = tiles.shape[1]
    far_per = n_rows // n_cols
    packed = pack(tiles, tile_rows, tile_cols, counts)
    set_len = packed.shape[0]

    perm = []
    for q in range(n_rows):
        for gp in range(n_cols):
            dst_r = gp * far_per + q % far_per
            dst_c = q // far_per
            perm.append((q * n_cols + gp, dst_r * n_cols + dst_c))
    moved = lax.ppermute(packed, ("rows", "cols"), perm)
    far = lax.all_gather(moved[None], "rows", axis=0, tiled=True)
    own = lax.all_gather(packed[None], "cols", axis=0, tiled=True)
    scal = lax.all_gather(scaling, "cols", axis=0, tiled=True).reshape(n_cols, CB_DEV, TB)

    own_meta = unpack_meta(own, slots)
    far_meta = unpack_meta(far, slots)
    out_cols = far_per * RB * TB

    grid_spec = pltpu.PrefetchScalarGridSpec(
        num_scalar_prefetch=2,
        grid=(n_cols,),
        in_specs=[
            pl.BlockSpec((1, set_len, TB), lambda g, om, fm: (g, 0, 0)),
            pl.BlockSpec((far_per, set_len, TB), lambda g, om, fm: (g, 0, 0)),
            pl.BlockSpec((1, CB_DEV, TB), lambda g, om, fm: (g, 0, 0)),
        ],
        out_specs=pl.BlockSpec((RB * TB, out_cols), lambda g, om, fm: (0, 0)),
        scratch_shapes=[
            pltpu.VMEM((RB * TB, CB_DEV * TB), jnp.float32),
            pltpu.VMEM((RB * TB, CB_DEV * TB), jnp.bfloat16),
            pltpu.VMEM((RB * TB, CB_DEV * TB), jnp.bfloat16),
        ],
    )
    return pl.pallas_call(
        functools.partial(normal_kernel, slots, far_per),
        grid_spec=grid_spec,
        out_shape=jax.ShapeDtypeStruct((RB * TB, out_cols), jnp.float32),
        compiler_params=pltpu.CompilerParams(dimension_semantics=("arbitrary",)),
    )(own_meta, far_meta, own, far, scal)


def solution(mesh):
    placed = (
        P("rows", "cols", None, None),
        P("rows", "cols"),
        P("rows", "cols"),
        P("rows", "cols"),
        P("cols"),
    )
    return jax.shard_map(
        per_device, mesh=mesh, in_specs=placed, out_specs=P("rows", "cols"), check_vma=False
    )
```

```python
import functools

import jax
import jax.numpy as jnp
from jax import lax
from jax.experimental import pallas as pl
from jax.experimental.pallas import tpu as pltpu
from jax.sharding import PartitionSpec as P

TB = 128
RB = 2
CB_DEV = 16
META = 8
MESH = pl.DeviceIdType.MESH


def pack(tiles, tile_rows, tile_cols, counts, scaling=None):
    slots = tiles.shape[1]
    meta = jnp.stack(
        [tile_rows[0], tile_cols[0], jnp.broadcast_to(counts[0, 0], (slots,))]
    ).astype(jnp.float32)
    meta = jnp.pad(meta, ((0, META - 3), (0, TB - slots)))
    parts = [tiles[0].reshape(slots * TB, TB), meta]
    if scaling is not None:
        parts += [scaling.reshape(CB_DEV, TB), jnp.zeros((META, TB), jnp.float32)]
    return jnp.concatenate(parts, axis=0)


def unpack_meta(sets, slots):
    return sets[:, slots * TB : slots * TB + 3, :slots].astype(jnp.int32).reshape(-1)


def ring_kernel(n, half, x_ref, out_ref, local_sem, send_sem, recv_sem):
    me = lax.axis_index("cols")
    row = lax.axis_index("rows")
    right = lax.rem(me + 1, n)
    left = lax.rem(me + n - 1, n)
    barrier = pltpu.get_barrier_semaphore()
    for neighbour in (left, right):
        pl.semaphore_signal(barrier, inc=1, device_id=(row, neighbour), device_id_type=MESH)
    pl.semaphore_wait(barrier, 2)

    local = pltpu.make_async_copy(x_ref, out_ref.at[me], local_sem)
    local.start()
    halves = (pl.ds(0, half), pl.ds(half, half))
    targets = (right, left)
    previous = [None, None]
    for step in range(n - 1):
        for way in range(2):
            if way == 0:
                origin = lax.rem(me - step + n, n)
            else:
                origin = lax.rem(me + step, n)
            if step == 0:
                src_ref = x_ref.at[halves[way]]
            else:
                previous[way].wait_recv()
                src_ref = out_ref.at[origin, halves[way]]
            copy = pltpu.make_async_remote_copy(
                src_ref=src_ref,
                dst_ref=out_ref.at[origin, halves[way]],
                send_sem=send_sem.at[way, step],
                recv_sem=recv_sem.at[way, step],
                device_id=(row, targets[way]),
                device_id_type=MESH,
            )
            copy.start()
            if previous[way] is not None:
                previous[way].wait_send()
            previous[way] = copy
    for way in range(2):
        previous[way].wait_recv()
        previous[way].wait_send()
    local.wait()


def ring_gather(x, n):
    rows = x.shape[0]
    return pl.pallas_call(
        functools.partial(ring_kernel, n, rows // 2),
        out_shape=jax.ShapeDtypeStruct((n,) + x.shape, x.dtype),
        in_specs=[pl.BlockSpec(memory_space=pl.ANY)],
        out_specs=pl.BlockSpec(memory_space=pl.ANY),
        scratch_shapes=[
            pltpu.SemaphoreType.DMA(()),
            pltpu.SemaphoreType.DMA((2, n - 1)),
            pltpu.SemaphoreType.DMA((2, n - 1)),
        ],
        compiler_params=pltpu.CompilerParams(collective_id=0, has_side_effects=True),
        cost_estimate=pl.CostEstimate(flops=0, bytes_accessed=2 * n * x.size * 4, transcendentals=0),
    )(x)


def split(x):
    hi = x.astype(jnp.bfloat16)
    lo = (x - hi.astype(jnp.float32)).astype(jnp.bfloat16)
    return hi, lo


def dot_t(a, b):
    return lax.dot_general(a, b, (((1,), (1,)), ((), ())), preferred_element_type=jnp.float32)


def normal_kernel(slots, far_per, own_meta, far_meta, own_ref, far_ref, out_ref, dense, p_hi, p_lo):
    g = pl.program_id(0)

    @pl.when(g == 0)
    def _():
        out_ref[...] = jnp.zeros_like(out_ref)

    dense[...] = jnp.zeros_like(dense)
    own_count = own_meta[(g * 3 + 2) * slots]
    for k in range(slots):

        @pl.when(k < own_count)
        def _():
            r = own_meta[(g * 3 + 0) * slots + k]
            c = own_meta[(g * 3 + 1) * slots + k]
            rows = pl.ds(pl.multiple_of(r * TB, TB), TB)
            cols = pl.ds(pl.multiple_of(c * TB, TB), TB)
            tile = own_ref[0, k * TB : (k + 1) * TB, :]
            dense[rows, cols] += tile * own_ref[0, pl.ds(slots * TB + META + c, 1), :]

    hi, lo = split(dense[...])
    p_hi[...] = hi
    p_lo[...] = lo

    def body(t, carry):
        qi = t // slots
        k = t % slots
        base = (g * far_per + qi) * 3 * slots
        count = far_meta[base + 2 * slots]

        @pl.when(k < count)
        def _():
            r = far_meta[base + k]
            c = far_meta[base + slots + k]
            cols = pl.ds(pl.multiple_of(c * TB, TB), TB)
            tile = far_ref[qi, pl.ds(pl.multiple_of(k * TB, TB), TB), :]
            t_hi, t_lo = split(tile)
            a_hi = p_hi[:, cols]
            a_lo = p_lo[:, cols]
            prod = dot_t(a_hi, t_hi) + (dot_t(a_hi, t_lo) + dot_t(a_lo, t_hi))
            dest = pl.ds(pl.multiple_of(qi * RB * TB + r * TB, TB), TB)
            out_ref[:, dest] += prod

        return carry

    lax.fori_loop(0, far_per * slots, body, 0)


def per_device(tiles, tile_rows, tile_cols, counts, scaling):
    n_rows = lax.axis_size("rows")
    n_cols = lax.axis_size("cols")
    slots = tiles.shape[1]
    far_per = n_rows // n_cols
    packed = pack(tiles, tile_rows, tile_cols, counts)
    set_len = packed.shape[0]
    own_packed = pack(tiles, tile_rows, tile_cols, counts, scaling)
    own_len = own_packed.shape[0]

    perm = []
    for q in range(n_rows):
        for gp in range(n_cols):
            dst_r = gp * far_per + q % far_per
            dst_c = q // far_per
            perm.append((q * n_cols + gp, dst_r * n_cols + dst_c))
    moved = lax.ppermute(packed, ("rows", "cols"), perm)
    far = lax.all_gather(moved[None], "rows", axis=0, tiled=True)
    own = ring_gather(own_packed, n_cols)

    own_meta = unpack_meta(own, slots)
    far_meta = unpack_meta(far, slots)
    out_cols = far_per * RB * TB

    grid_spec = pltpu.PrefetchScalarGridSpec(
        num_scalar_prefetch=2,
        grid=(n_cols,),
        in_specs=[
            pl.BlockSpec((1, own_len, TB), lambda g, om, fm: (g, 0, 0)),
            pl.BlockSpec((far_per, set_len, TB), lambda g, om, fm: (g, 0, 0)),
        ],
        out_specs=pl.BlockSpec((RB * TB, out_cols), lambda g, om, fm: (0, 0)),
        scratch_shapes=[
            pltpu.VMEM((RB * TB, CB_DEV * TB), jnp.float32),
            pltpu.VMEM((RB * TB, CB_DEV * TB), jnp.bfloat16),
            pltpu.VMEM((RB * TB, CB_DEV * TB), jnp.bfloat16),
        ],
    )
    return pl.pallas_call(
        functools.partial(normal_kernel, slots, far_per),
        grid_spec=grid_spec,
        out_shape=jax.ShapeDtypeStruct((RB * TB, out_cols), jnp.float32),
        compiler_params=pltpu.CompilerParams(dimension_semantics=("arbitrary",)),
    )(own_meta, far_meta, own, far)


def solution(mesh):
    placed = (
        P("rows", "cols", None, None),
        P("rows", "cols"),
        P("rows", "cols"),
        P("rows", "cols"),
        P("cols"),
    )
    return jax.shard_map(
        per_device, mesh=mesh, in_specs=placed, out_specs=P("rows", "cols"), check_vma=False
    )
```

```python
import functools

import jax
import jax.numpy as jnp
from jax import lax
from jax.experimental import pallas as pl
from jax.experimental.pallas import tpu as pltpu
from jax.sharding import PartitionSpec as P

TB = 128
RB = 2
CB_DEV = 16
META = 8
MESH = pl.DeviceIdType.MESH


def pack(tiles, tile_rows, tile_cols, counts, scaling=None):
    slots = tiles.shape[1]
    meta = jnp.stack(
        [tile_rows[0], tile_cols[0], jnp.broadcast_to(counts[0, 0], (slots,))]
    ).astype(jnp.float32)
    meta = jnp.pad(meta, ((0, META - 3), (0, TB - slots)))
    parts = [tiles[0].reshape(slots * TB, TB), meta]
    if scaling is not None:
        parts += [scaling.reshape(CB_DEV, TB), jnp.zeros((META, TB), jnp.float32)]
    return jnp.concatenate(parts, axis=0)


def unpack_meta(sets, slots):
    return sets[:, slots * TB : slots * TB + 3, :slots].astype(jnp.int32).reshape(-1)


def ring_kernel(n, half, x_ref, out_ref, local_sem, send_sem, recv_sem):
    me = lax.axis_index("cols")
    row = lax.axis_index("rows")
    right = lax.rem(me + 1, n)
    left = lax.rem(me + n - 1, n)
    barrier = pltpu.get_barrier_semaphore()
    for neighbour in (left, right):
        pl.semaphore_signal(barrier, inc=1, device_id=(row, neighbour), device_id_type=MESH)
    pl.semaphore_wait(barrier, 2)

    local = pltpu.make_async_copy(x_ref, out_ref.at[me], local_sem)
    local.start()
    halves = (pl.ds(0, half), pl.ds(half, half))
    targets = (right, left)
    previous = [None, None]
    for step in range(n - 1):
        for way in range(2):
            if way == 0:
                origin = lax.rem(me - step + n, n)
            else:
                origin = lax.rem(me + step, n)
            if step == 0:
                src_ref = x_ref.at[halves[way]]
            else:
                previous[way].wait_recv()
                src_ref = out_ref.at[origin, halves[way]]
            copy = pltpu.make_async_remote_copy(
                src_ref=src_ref,
                dst_ref=out_ref.at[origin, halves[way]],
                send_sem=send_sem.at[way, step],
                recv_sem=recv_sem.at[way, step],
                device_id=(row, targets[way]),
                device_id_type=MESH,
            )
            copy.start()
            if previous[way] is not None:
                previous[way].wait_send()
            previous[way] = copy
    for way in range(2):
        previous[way].wait_recv()
        previous[way].wait_send()
    local.wait()


def ring_gather(x, n):
    rows = x.shape[0]
    return pl.pallas_call(
        functools.partial(ring_kernel, n, rows // 2),
        out_shape=jax.ShapeDtypeStruct((n,) + x.shape, x.dtype),
        in_specs=[pl.BlockSpec(memory_space=pl.ANY)],
        out_specs=pl.BlockSpec(memory_space=pl.ANY),
        scratch_shapes=[
            pltpu.SemaphoreType.DMA(()),
            pltpu.SemaphoreType.DMA((2, n - 1)),
            pltpu.SemaphoreType.DMA((2, n - 1)),
        ],
        compiler_params=pltpu.CompilerParams(collective_id=0, has_side_effects=True),
        cost_estimate=pl.CostEstimate(flops=0, bytes_accessed=2 * n * x.size * 4, transcendentals=0),
    )(x)


def split(x):
    hi = x.astype(jnp.bfloat16)
    lo = (x - hi.astype(jnp.float32)).astype(jnp.bfloat16)
    return hi, lo


def dot_t(a, b):
    return lax.dot_general(a, b, (((1,), (1,)), ((), ())), preferred_element_type=jnp.float32)


def normal_kernel(slots, far_per, own_meta, far_meta, own_ref, far_ref, out_ref, dense, p_hi, p_lo, x_hi, x_lo, z_hi, z_lo):
    g = pl.program_id(0)

    @pl.when(g == 0)
    def _():
        out_ref[...] = jnp.zeros_like(out_ref)

    dense[...] = jnp.zeros_like(dense)
    own_count = own_meta[(g * 3 + 2) * slots]
    for k in range(slots):

        @pl.when(k < own_count)
        def _():
            r = own_meta[(g * 3 + 0) * slots + k]
            c = own_meta[(g * 3 + 1) * slots + k]
            rows = pl.ds(pl.multiple_of(r * TB, TB), TB)
            cols = pl.ds(pl.multiple_of(c * TB, TB), TB)
            tile = own_ref[0, k * TB : (k + 1) * TB, :]
            dense[rows, cols] += tile * own_ref[0, pl.ds(slots * TB + META + c, 1), :]

    hi, lo = split(dense[...])
    p_hi[...] = hi
    p_lo[...] = lo

    for qi in range(far_per):
        base = (g * far_per + qi) * 3 * slots
        count = far_meta[base + 2 * slots]
        for k in range(slots):
            r = far_meta[base + k]
            c = jnp.minimum(jnp.maximum(far_meta[base + slots + k], 0), CB_DEV - 1)
            src = pl.ds(pl.multiple_of(c * TB, TB), TB)
            x_hi[:, k * TB : (k + 1) * TB] = p_hi[:, src]
            x_lo[:, k * TB : (k + 1) * TB] = p_lo[:, src]
            t_hi, t_lo = split(far_ref[qi, k * TB : (k + 1) * TB, :])
            live = k < count
            for half in range(RB):
                keep = jnp.logical_and(live, r == half)
                z_hi[half * TB : (half + 1) * TB, k * TB : (k + 1) * TB] = jnp.where(keep, t_hi, jnp.zeros_like(t_hi))
                z_lo[half * TB : (half + 1) * TB, k * TB : (k + 1) * TB] = jnp.where(keep, t_lo, jnp.zeros_like(t_lo))
        a_hi = x_hi[...]
        b_hi = z_hi[...]
        prod = dot_t(a_hi, b_hi) + (dot_t(a_hi, z_lo[...]) + dot_t(x_lo[...], b_hi))
        out_ref[:, qi * RB * TB : (qi + 1) * RB * TB] += prod


def per_device(tiles, tile_rows, tile_cols, counts, scaling):
    n_rows = lax.axis_size("rows")
    n_cols = lax.axis_size("cols")
    slots = tiles.shape[1]
    far_per = n_rows // n_cols
    packed = pack(tiles, tile_rows, tile_cols, counts)
    set_len = packed.shape[0]
    own_packed = pack(tiles, tile_rows, tile_cols, counts, scaling)
    own_len = own_packed.shape[0]

    perm = []
    for q in range(n_rows):
        for gp in range(n_cols):
            dst_r = gp * far_per + q % far_per
            dst_c = q // far_per
            perm.append((q * n_cols + gp, dst_r * n_cols + dst_c))
    moved = lax.ppermute(packed, ("rows", "cols"), perm)
    far = lax.all_gather(moved[None], "rows", axis=0, tiled=True)
    own = ring_gather(own_packed, n_cols)

    own_meta = unpack_meta(own, slots)
    far_meta = unpack_meta(far, slots)
    out_cols = far_per * RB * TB

    grid_spec = pltpu.PrefetchScalarGridSpec(
        num_scalar_prefetch=2,
        grid=(n_cols,),
        in_specs=[
            pl.BlockSpec((1, own_len, TB), lambda g, om, fm: (g, 0, 0)),
            pl.BlockSpec((far_per, set_len, TB), lambda g, om, fm: (g, 0, 0)),
        ],
        out_specs=pl.BlockSpec((RB * TB, out_cols), lambda g, om, fm: (0, 0)),
        scratch_shapes=[
            pltpu.VMEM((RB * TB, CB_DEV * TB), jnp.float32),
            pltpu.VMEM((RB * TB, CB_DEV * TB), jnp.bfloat16),
            pltpu.VMEM((RB * TB, CB_DEV * TB), jnp.bfloat16),
            pltpu.VMEM((RB * TB, slots * TB), jnp.bfloat16),
            pltpu.VMEM((RB * TB, slots * TB), jnp.bfloat16),
            pltpu.VMEM((RB * TB, slots * TB), jnp.bfloat16),
            pltpu.VMEM((RB * TB, slots * TB), jnp.bfloat16),
        ],
    )
    return pl.pallas_call(
        functools.partial(normal_kernel, slots, far_per),
        grid_spec=grid_spec,
        out_shape=jax.ShapeDtypeStruct((RB * TB, out_cols), jnp.float32),
        compiler_params=pltpu.CompilerParams(dimension_semantics=("arbitrary",)),
    )(own_meta, far_meta, own, far)


def solution(mesh):
    placed = (
        P("rows", "cols", None, None),
        P("rows", "cols"),
        P("rows", "cols"),
        P("rows", "cols"),
        P("cols"),
    )
    return jax.shard_map(
        per_device, mesh=mesh, in_specs=placed, out_specs=P("rows", "cols"), check_vma=False
    )
```

```python
import functools

import jax
import jax.numpy as jnp
from jax import lax
from jax.experimental import pallas as pl
from jax.experimental.pallas import tpu as pltpu
from jax.sharding import PartitionSpec as P

TB = 128
RB = 2
CB_DEV = 16
META = 8
MESH = pl.DeviceIdType.MESH
ROW_AXES = ("y", "x", "c")


def pack(tiles, tile_rows, tile_cols, counts, scaling=None):
    slots = tiles.shape[1]
    meta = jnp.stack(
        [tile_rows[0], tile_cols[0], jnp.broadcast_to(counts[0, 0], (slots,))]
    ).astype(jnp.float32)
    meta = jnp.pad(meta, ((0, META - 3), (0, TB - slots)))
    parts = [tiles[0].reshape(slots * TB, TB), meta]
    if scaling is not None:
        parts += [scaling.reshape(CB_DEV, TB), jnp.zeros((META, TB), jnp.float32)]
    return jnp.concatenate(parts, axis=0)


def unpack_meta(sets, slots):
    return sets[:, slots * TB : slots * TB + 3, :slots].astype(jnp.int32).reshape(-1)


def ring_kernel(n, half, x_ref, out_ref, local_sem, send_sem, recv_sem):
    me = lax.axis_index("z")
    here = tuple(lax.axis_index(a) for a in ROW_AXES)
    right = lax.rem(me + 1, n)
    left = lax.rem(me + n - 1, n)
    barrier = pltpu.get_barrier_semaphore()
    for neighbour in (left, right):
        pl.semaphore_signal(barrier, inc=1, device_id=here + (neighbour,), device_id_type=MESH)
    pl.semaphore_wait(barrier, 2)

    local = pltpu.make_async_copy(x_ref, out_ref.at[me], local_sem)
    local.start()
    halves = (pl.ds(0, half), pl.ds(half, half))
    targets = (right, left)
    previous = [None, None]
    for step in range(n - 1):
        for way in range(2):
            if way == 0:
                origin = lax.rem(me - step + n, n)
            else:
                origin = lax.rem(me + step, n)
            if step == 0:
                src_ref = x_ref.at[halves[way]]
            else:
                previous[way].wait_recv()
                src_ref = out_ref.at[origin, halves[way]]
            copy = pltpu.make_async_remote_copy(
                src_ref=src_ref,
                dst_ref=out_ref.at[origin, halves[way]],
                send_sem=send_sem.at[way, step],
                recv_sem=recv_sem.at[way, step],
                device_id=here + (targets[way],),
                device_id_type=MESH,
            )
            copy.start()
            if previous[way] is not None:
                previous[way].wait_send()
            previous[way] = copy
    for way in range(2):
        previous[way].wait_recv()
        previous[way].wait_send()
    local.wait()


def ring_gather(x, n):
    rows = x.shape[0]
    return pl.pallas_call(
        functools.partial(ring_kernel, n, rows // 2),
        out_shape=jax.ShapeDtypeStruct((n,) + x.shape, x.dtype),
        in_specs=[pl.BlockSpec(memory_space=pl.ANY)],
        out_specs=pl.BlockSpec(memory_space=pl.ANY),
        scratch_shapes=[
            pltpu.SemaphoreType.DMA(()),
            pltpu.SemaphoreType.DMA((2, n - 1)),
            pltpu.SemaphoreType.DMA((2, n - 1)),
        ],
        compiler_params=pltpu.CompilerParams(collective_id=0, has_side_effects=True),
        cost_estimate=pl.CostEstimate(flops=0, bytes_accessed=2 * n * x.size * 4, transcendentals=0),
    )(x)


def split(x):
    hi = x.astype(jnp.bfloat16)
    lo = (x - hi.astype(jnp.float32)).astype(jnp.bfloat16)
    return hi, lo


def dot_t(a, b):
    return lax.dot_general(a, b, (((1,), (1,)), ((), ())), preferred_element_type=jnp.float32)


def normal_kernel(slots, far_per, own_meta, far_meta, own_ref, far_ref, out_ref, dense, p_hi, p_lo, x_hi, x_lo, z_hi, z_lo):
    g = pl.program_id(0)

    @pl.when(g == 0)
    def _():
        out_ref[...] = jnp.zeros_like(out_ref)

    dense[...] = jnp.zeros_like(dense)
    own_count = own_meta[(g * 3 + 2) * slots]
    for k in range(slots):

        @pl.when(k < own_count)
        def _():
            r = own_meta[(g * 3 + 0) * slots + k]
            c = own_meta[(g * 3 + 1) * slots + k]
            rows = pl.ds(pl.multiple_of(r * TB, TB), TB)
            cols = pl.ds(pl.multiple_of(c * TB, TB), TB)
            tile = own_ref[0, k * TB : (k + 1) * TB, :]
            dense[rows, cols] += tile * own_ref[0, pl.ds(slots * TB + META + c, 1), :]

    hi, lo = split(dense[...])
    p_hi[...] = hi
    p_lo[...] = lo

    for qi in range(far_per):
        base = (g * far_per + qi) * 3 * slots
        count = far_meta[base + 2 * slots]
        for k in range(slots):
            r = far_meta[base + k]
            c = jnp.minimum(jnp.maximum(far_meta[base + slots + k], 0), CB_DEV - 1)
            src = pl.ds(pl.multiple_of(c * TB, TB), TB)
            x_hi[:, k * TB : (k + 1) * TB] = p_hi[:, src]
            x_lo[:, k * TB : (k + 1) * TB] = p_lo[:, src]
            t_hi, t_lo = split(far_ref[qi, k * TB : (k + 1) * TB, :])
            live = k < count
            for half in range(RB):
                keep = jnp.logical_and(live, r == half)
                z_hi[half * TB : (half + 1) * TB, k * TB : (k + 1) * TB] = jnp.where(keep, t_hi, jnp.zeros_like(t_hi))
                z_lo[half * TB : (half + 1) * TB, k * TB : (k + 1) * TB] = jnp.where(keep, t_lo, jnp.zeros_like(t_lo))
        a_hi = x_hi[...]
        b_hi = z_hi[...]
        prod = dot_t(a_hi, b_hi) + (dot_t(a_hi, z_lo[...]) + dot_t(x_lo[...], b_hi))
        out_ref[:, qi * RB * TB : (qi + 1) * RB * TB] += prod


def per_device(tiles, tile_rows, tile_cols, counts, scaling):
    n_rows = lax.axis_size(ROW_AXES)
    n_cols = lax.axis_size("z")
    slots = tiles.shape[1]
    far_per = n_rows // n_cols
    packed = pack(tiles, tile_rows, tile_cols, counts)
    set_len = packed.shape[0]
    own_packed = pack(tiles, tile_rows, tile_cols, counts, scaling)
    own_len = own_packed.shape[0]

    perm = []
    for q in range(n_rows):
        for gp in range(n_cols):
            dst_r = gp * far_per + q % far_per
            dst_c = q // far_per
            perm.append((q * n_cols + gp, dst_r * n_cols + dst_c))
    moved = lax.ppermute(packed, ROW_AXES + ("z",), perm)
    far = lax.all_gather(moved[None], ("y", "x"), axis=0, tiled=True)
    far = lax.all_gather(far, "c", axis=1, tiled=False)
    far = far.reshape((n_rows,) + moved.shape)
    own = ring_gather(own_packed, n_cols)

    own_meta = unpack_meta(own, slots)
    far_meta = unpack_meta(far, slots)
    out_cols = far_per * RB * TB

    grid_spec = pltpu.PrefetchScalarGridSpec(
        num_scalar_prefetch=2,
        grid=(n_cols,),
        in_specs=[
            pl.BlockSpec((1, own_len, TB), lambda g, om, fm: (g, 0, 0)),
            pl.BlockSpec((far_per, set_len, TB), lambda g, om, fm: (g, 0, 0)),
        ],
        out_specs=pl.BlockSpec((RB * TB, out_cols), lambda g, om, fm: (0, 0)),
        scratch_shapes=[
            pltpu.VMEM((RB * TB, CB_DEV * TB), jnp.float32),
            pltpu.VMEM((RB * TB, CB_DEV * TB), jnp.bfloat16),
            pltpu.VMEM((RB * TB, CB_DEV * TB), jnp.bfloat16),
            pltpu.VMEM((RB * TB, slots * TB), jnp.bfloat16),
            pltpu.VMEM((RB * TB, slots * TB), jnp.bfloat16),
            pltpu.VMEM((RB * TB, slots * TB), jnp.bfloat16),
            pltpu.VMEM((RB * TB, slots * TB), jnp.bfloat16),
        ],
    )
    return pl.pallas_call(
        functools.partial(normal_kernel, slots, far_per),
        grid_spec=grid_spec,
        out_shape=jax.ShapeDtypeStruct((RB * TB, out_cols), jnp.float32),
        compiler_params=pltpu.CompilerParams(dimension_semantics=("arbitrary",)),
    )(own_meta, far_meta, own, far)


def solution(mesh):
    n_rows, n_cols = mesh.devices.shape
    split_mesh = jax.sharding.Mesh(mesh.devices.reshape(n_rows // 8, 4, 2, n_cols), ROW_AXES + ("z",))
    placed = (
        P(ROW_AXES, "z", None, None),
        P(ROW_AXES, "z"),
        P(ROW_AXES, "z"),
        P(ROW_AXES, "z"),
        P("z"),
    )
    return jax.shard_map(
        per_device, mesh=split_mesh, in_specs=placed, out_specs=P(ROW_AXES, "z"), check_vma=False
    )
```

```python
import functools

import jax
import jax.numpy as jnp
from jax import lax
from jax.experimental import pallas as pl
from jax.experimental.pallas import tpu as pltpu
from jax.sharding import PartitionSpec as P

TB = 128
RB = 2
CB_DEV = 16
META = 8
MESH = pl.DeviceIdType.MESH


def pack(tiles, tile_rows, tile_cols, counts, scaling=None):
    slots = tiles.shape[1]
    meta = jnp.stack(
        [tile_rows[0], tile_cols[0], jnp.broadcast_to(counts[0, 0], (slots,))]
    ).astype(jnp.float32)
    meta = jnp.pad(meta, ((0, META - 3), (0, TB - slots)))
    parts = [tiles[0].reshape(slots * TB, TB), meta]
    if scaling is not None:
        parts += [scaling.reshape(CB_DEV, TB), jnp.zeros((META, TB), jnp.float32)]
    return jnp.concatenate(parts, axis=0)


def unpack_meta(sets, slots):
    return sets[:, slots * TB : slots * TB + 3, :slots].astype(jnp.int32).reshape(-1)


def comm_kernel(n, side, own_half, far_half, own_x, far_x, own_out, far_out, sems, z_send, z_recv, f_send, f_recv, p_send, p_recv):
    me = lax.axis_index("cols")
    row = lax.axis_index("rows")
    core = row % 2
    y = row // (2 * side)
    x = (row // 2) % side
    step_a = (core, 1 - core)
    step_b = (1 - core, core)

    def spot(da, db, cc):
        yy = (y + da * step_a[0] + db * step_b[0] + 2 * side) % side
        xx = (x + da * step_a[1] + db * step_b[1] + 2 * side) % side
        return (yy * side + xx) * 2 + cc

    z_right = lax.rem(me + 1, n)
    z_left = lax.rem(me + n - 1, n)
    partner = row - core + (1 - core)
    barrier = pltpu.get_barrier_semaphore()
    peers = [(row, z_left), (row, z_right), (partner, me)]
    for s in (1, -1):
        peers.append((spot(s, 0, core), me))
        peers.append((spot(0, s, core), me))
    for peer in peers:
        pl.semaphore_signal(barrier, inc=1, device_id=peer, device_id_type=MESH)
    pl.semaphore_wait(barrier, len(peers))

    local_own = pltpu.make_async_copy(own_x, own_out.at[me], sems.at[0])
    local_own.start()
    local_far = pltpu.make_async_copy(far_x, far_out.at[spot(0, 0, core)], sems.at[1])
    local_far.start()

    far_rows = far_x.shape[0]
    halves = (pl.ds(0, far_half), pl.ds(far_half, far_rows - far_half))
    started = []
    partner_copies = []

    def send(src, dst, sem_s, sem_r, peer):
        copy = pltpu.make_async_remote_copy(
            src_ref=src, dst_ref=dst, send_sem=sem_s, recv_sem=sem_r, device_id=peer, device_id_type=MESH
        )
        copy.start()
        started.append(copy)
        return copy

    def to_partner(slot, src=None):
        j = len(partner_copies)
        src = far_out.at[slot] if src is None else src
        partner_copies.append(send(src, far_out.at[slot], p_send.at[j], p_recv.at[j], (partner, me)))

    own_halves = (pl.ds(0, own_half), pl.ds(own_half, own_half))
    z_prev = [None, None]

    def z_step(step):
        if step >= n - 1:
            return
        for way in range(2):
            if way == 0:
                origin = lax.rem(me - step + n, n)
            else:
                origin = lax.rem(me + step, n)
            if step == 0:
                src = own_x.at[own_halves[way]]
            else:
                z_prev[way].wait_recv()
                src = own_out.at[origin, own_halves[way]]
            z_prev[way] = send(
                src, own_out.at[origin, own_halves[way]], z_send.at[way, step], z_recv.at[way, step],
                (row, (z_right, z_left)[way]),
            )

    z_step(0)
    to_partner(spot(0, 0, core), far_x)
    first = [send(far_x, far_out.at[spot(0, 0, core)], f_send.at[0, w], f_recv.at[0, w], (spot(s, 0, core), me))
             for w, s in enumerate((1, -1))]
    for copy in first:
        copy.wait_recv()
    to_partner(spot(-1, 0, core))
    to_partner(spot(1, 0, core))
    second = [send(far_out.at[spot(-s, 0, core), halves[w]], far_out.at[spot(-s, 0, core), halves[w]],
                   f_send.at[1, w], f_recv.at[1, w], (spot(s, 0, core), me))
              for w, s in enumerate((1, -1))]
    z_step(1)
    for copy in second:
        copy.wait_recv()
    to_partner(spot(2, 0, core))
    held = (0, -1, 1, 2)
    third = []
    for w, s in enumerate((1, -1)):
        for i, da in enumerate(held):
            slot = spot(da, 0, core)
            third.append(send(far_x if da == 0 else far_out.at[slot], far_out.at[slot], f_send.at[2 + w, i], f_recv.at[2 + w, i],
                              (spot(0, s, core), me)))
    z_step(2)
    for copy in third:
        copy.wait_recv()
    for s in (1, -1):
        for da in held:
            to_partner(spot(da, -s, core))
    fourth = []
    for w, s in enumerate((1, -1)):
        for i, da in enumerate(held):
            slot = spot(da, -s, core)
            fourth.append(send(far_out.at[slot, halves[w]], far_out.at[slot, halves[w]],
                               f_send.at[4 + w, i], f_recv.at[4 + w, i], (spot(0, s, core), me)))
    z_step(3)
    for copy in fourth:
        copy.wait_recv()
    for da in held:
        to_partner(spot(da, 2, core))
    for step in range(4, n - 1):
        z_step(step)
    for way in range(2):
        z_prev[way].wait_recv()
    for copy in partner_copies:
        copy.wait_recv()
    for copy in started:
        copy.wait_send()
    local_own.wait()
    local_far.wait()


def gather_all(own_x, far_x, n, n_far):
    side = 4
    return pl.pallas_call(
        functools.partial(comm_kernel, n, side, own_x.shape[0] // 2, 512),
        out_shape=(
            jax.ShapeDtypeStruct((n,) + own_x.shape, own_x.dtype),
            jax.ShapeDtypeStruct((n_far,) + far_x.shape, far_x.dtype),
        ),
        in_specs=[pl.BlockSpec(memory_space=pl.ANY)] * 2,
        out_specs=(pl.BlockSpec(memory_space=pl.ANY), pl.BlockSpec(memory_space=pl.ANY)),
        scratch_shapes=[
            pltpu.SemaphoreType.DMA((2,)),
            pltpu.SemaphoreType.DMA((2, n - 1)),
            pltpu.SemaphoreType.DMA((2, n - 1)),
            pltpu.SemaphoreType.DMA((6, 4)),
            pltpu.SemaphoreType.DMA((6, 4)),
            pltpu.SemaphoreType.DMA((n_far // 2,)),
            pltpu.SemaphoreType.DMA((n_far // 2,)),
        ],
        compiler_params=pltpu.CompilerParams(collective_id=0, has_side_effects=True),
    )(own_x, far_x)


def split(x):
    hi = x.astype(jnp.bfloat16)
    lo = (x - hi.astype(jnp.float32)).astype(jnp.bfloat16)
    return hi, lo


def dot_t(a, b):
    return lax.dot_general(a, b, (((1,), (1,)), ((), ())), preferred_element_type=jnp.float32)


def normal_kernel(slots, far_per, own_meta, far_meta, own_ref, far_ref, out_ref, dense, p_hi, p_lo, x_hi, x_lo, z_hi, z_lo):
    g = pl.program_id(0)

    @pl.when(g == 0)
    def _():
        out_ref[...] = jnp.zeros_like(out_ref)

    dense[...] = jnp.zeros_like(dense)
    own_count = own_meta[(g * 3 + 2) * slots]
    for k in range(slots):

        @pl.when(k < own_count)
        def _():
            r = own_meta[(g * 3 + 0) * slots + k]
            c = own_meta[(g * 3 + 1) * slots + k]
            rows = pl.ds(pl.multiple_of(r * TB, TB), TB)
            cols = pl.ds(pl.multiple_of(c * TB, TB), TB)
            tile = own_ref[0, k * TB : (k + 1) * TB, :]
            dense[rows, cols] += tile * own_ref[0, pl.ds(slots * TB + META + c, 1), :]

    hi, lo = split(dense[...])
    p_hi[...] = hi
    p_lo[...] = lo

    for qi in range(far_per):
        base = (g * far_per + qi) * 3 * slots
        count = far_meta[base + 2 * slots]
        for k in range(slots):
            r = far_meta[base + k]
            c = jnp.minimum(jnp.maximum(far_meta[base + slots + k], 0), CB_DEV - 1)
            src = pl.ds(pl.multiple_of(c * TB, TB), TB)
            x_hi[:, k * TB : (k + 1) * TB] = p_hi[:, src]
            x_lo[:, k * TB : (k + 1) * TB] = p_lo[:, src]
            t_hi, t_lo = split(far_ref[qi, k * TB : (k + 1) * TB, :])
            live = k < count
            for half in range(RB):
                keep = jnp.logical_and(live, r == half)
                z_hi[half * TB : (half + 1) * TB, k * TB : (k + 1) * TB] = jnp.where(keep, t_hi, jnp.zeros_like(t_hi))
                z_lo[half * TB : (half + 1) * TB, k * TB : (k + 1) * TB] = jnp.where(keep, t_lo, jnp.zeros_like(t_lo))
        a_hi = x_hi[...]
        b_hi = z_hi[...]
        prod = dot_t(a_hi, b_hi) + (dot_t(a_hi, z_lo[...]) + dot_t(x_lo[...], b_hi))
        out_ref[:, qi * RB * TB : (qi + 1) * RB * TB] += prod


def per_device(tiles, tile_rows, tile_cols, counts, scaling):
    n_rows = lax.axis_size("rows")
    n_cols = lax.axis_size("cols")
    slots = tiles.shape[1]
    far_per = n_rows // n_cols
    packed = pack(tiles, tile_rows, tile_cols, counts)
    set_len = packed.shape[0]
    own_packed = pack(tiles, tile_rows, tile_cols, counts, scaling)
    own_len = own_packed.shape[0]

    perm = []
    for q in range(n_rows):
        for gp in range(n_cols):
            dst_r = gp * far_per + q % far_per
            dst_c = q // far_per
            perm.append((q * n_cols + gp, dst_r * n_cols + dst_c))
    moved = lax.ppermute(packed, ("rows", "cols"), perm)
    own, far = gather_all(own_packed, moved, n_cols, n_rows)

    own_meta = unpack_meta(own, slots)
    far_meta = unpack_meta(far, slots)
    out_cols = far_per * RB * TB

    grid_spec = pltpu.PrefetchScalarGridSpec(
        num_scalar_prefetch=2,
        grid=(n_cols,),
        in_specs=[
            pl.BlockSpec((1, own_len, TB), lambda g, om, fm: (g, 0, 0)),
            pl.BlockSpec((far_per, set_len, TB), lambda g, om, fm: (g, 0, 0)),
        ],
        out_specs=pl.BlockSpec((RB * TB, out_cols), lambda g, om, fm: (0, 0)),
        scratch_shapes=[
            pltpu.VMEM((RB * TB, CB_DEV * TB), jnp.float32),
            pltpu.VMEM((RB * TB, CB_DEV * TB), jnp.bfloat16),
            pltpu.VMEM((RB * TB, CB_DEV * TB), jnp.bfloat16),
            pltpu.VMEM((RB * TB, slots * TB), jnp.bfloat16),
            pltpu.VMEM((RB * TB, slots * TB), jnp.bfloat16),
            pltpu.VMEM((RB * TB, slots * TB), jnp.bfloat16),
            pltpu.VMEM((RB * TB, slots * TB), jnp.bfloat16),
        ],
    )
    return pl.pallas_call(
        functools.partial(normal_kernel, slots, far_per),
        grid_spec=grid_spec,
        out_shape=jax.ShapeDtypeStruct((RB * TB, out_cols), jnp.float32),
        compiler_params=pltpu.CompilerParams(dimension_semantics=("arbitrary",)),
    )(own_meta, far_meta, own, far)


def solution(mesh):
    placed = (
        P("rows", "cols", None, None),
        P("rows", "cols"),
        P("rows", "cols"),
        P("rows", "cols"),
        P("cols"),
    )
    return jax.shard_map(
        per_device, mesh=mesh, in_specs=placed, out_specs=P("rows", "cols"), check_vma=False
    )
```

```python
import functools

import jax
import jax.numpy as jnp
from jax import lax
from jax.experimental import pallas as pl
from jax.experimental.pallas import tpu as pltpu
from jax.sharding import PartitionSpec as P

TB = 128
RB = 2
CB_DEV = 16
META = 8
MESH = pl.DeviceIdType.MESH


def pack(tiles, tile_rows, tile_cols, counts, scaling=None):
    slots = tiles.shape[1]
    meta = jnp.stack(
        [tile_rows[0], tile_cols[0], jnp.broadcast_to(counts[0, 0], (slots,))]
    ).astype(jnp.float32)
    meta = jnp.pad(meta, ((0, META - 3), (0, TB - slots)))
    parts = [tiles[0].reshape(slots * TB, TB), meta]
    if scaling is not None:
        parts += [scaling.reshape(CB_DEV, TB), jnp.zeros((META, TB), jnp.float32)]
    return jnp.concatenate(parts, axis=0)


def unpack_meta(sets, slots):
    return sets[:, slots * TB : slots * TB + 3, :slots].astype(jnp.int32).reshape(-1)


def comm_kernel(n, side, own_half, far_half, own_x, far_x, own_out, far_out, sems, z_send, z_recv, f_send, f_recv, p_send, p_recv):
    me = lax.axis_index("cols")
    row = lax.axis_index("rows")
    core = row % 2
    y = row // (2 * side)
    x = (row // 2) % side
    step_a = (core, 1 - core)
    step_b = (1 - core, core)

    def spot(da, db, cc):
        yy = (y + da * step_a[0] + db * step_b[0] + 2 * side) % side
        xx = (x + da * step_a[1] + db * step_b[1] + 2 * side) % side
        return (yy * side + xx) * 2 + cc

    z_right = lax.rem(me + 1, n)
    z_left = lax.rem(me + n - 1, n)
    partner = row - core + (1 - core)
    far_per = far_out.shape[0] // n
    dest = (lax.rem(me + 1, n) * far_per + row % far_per, row // far_per)
    origin_plane = lax.rem(row // far_per + n - 1, n)
    source = (me * far_per + row % far_per, origin_plane)
    barrier = pltpu.get_barrier_semaphore()
    peers = [(row, z_left), (row, z_right), (partner, me), dest, source]
    for s in (1, -1):
        peers.append((spot(s, 0, core), me))
        peers.append((spot(0, s, core), me))
    for peer in peers:
        pl.semaphore_signal(barrier, inc=1, device_id=peer, device_id_type=MESH)
    pl.semaphore_wait(barrier, len(peers))

    local_own = pltpu.make_async_copy(own_x, own_out.at[me], sems.at[0])
    local_own.start()

    far_rows = far_x.shape[0]
    halves = (pl.ds(0, far_half), pl.ds(far_half, far_rows - far_half))
    started = []
    partner_copies = []

    def send(src, dst, sem_s, sem_r, peer):
        copy = pltpu.make_async_remote_copy(
            src_ref=src, dst_ref=dst, send_sem=sem_s, recv_sem=sem_r, device_id=peer, device_id_type=MESH
        )
        copy.start()
        started.append(copy)
        return copy

    def to_partner(slot, src=None):
        j = len(partner_copies)
        src = far_out.at[slot] if src is None else src
        partner_copies.append(send(src, far_out.at[slot], p_send.at[j], p_recv.at[j], (partner, me)))

    own_halves = (pl.ds(0, own_half), pl.ds(own_half, own_half))
    z_prev = [None, None]

    def z_step(step):
        if step >= n - 1:
            return
        for way in range(2):
            if way == 0:
                origin = lax.rem(me - step + n, n)
            else:
                origin = lax.rem(me + step, n)
            if step == 0:
                src = own_x.at[own_halves[way]]
            else:
                z_prev[way].wait_recv()
                src = own_out.at[origin, own_halves[way]]
            z_prev[way] = send(
                src, own_out.at[origin, own_halves[way]], z_send.at[way, step], z_recv.at[way, step],
                (row, (z_right, z_left)[way]),
            )

    z_step(0)
    moved = send(far_x, far_out.at[dest[0]], sems.at[1], sems.at[2], dest)
    moved.wait_recv()
    to_partner(spot(0, 0, core))
    first = [send(far_out.at[spot(0, 0, core)], far_out.at[spot(0, 0, core)], f_send.at[0, w], f_recv.at[0, w], (spot(s, 0, core), me))
             for w, s in enumerate((1, -1))]
    for copy in first:
        copy.wait_recv()
    to_partner(spot(-1, 0, core))
    to_partner(spot(1, 0, core))
    second = [send(far_out.at[spot(-s, 0, core), halves[w]], far_out.at[spot(-s, 0, core), halves[w]],
                   f_send.at[1, w], f_recv.at[1, w], (spot(s, 0, core), me))
              for w, s in enumerate((1, -1))]
    z_step(1)
    for copy in second:
        copy.wait_recv()
    to_partner(spot(2, 0, core))
    held = (0, -1, 1, 2)
    third = []
    for w, s in enumerate((1, -1)):
        for i, da in enumerate(held):
            slot = spot(da, 0, core)
            third.append(send(far_out.at[slot], far_out.at[slot], f_send.at[2 + w, i], f_recv.at[2 + w, i],
                              (spot(0, s, core), me)))
    z_step(2)
    for copy in third:
        copy.wait_recv()
    for s in (1, -1):
        for da in held:
            to_partner(spot(da, -s, core))
    fourth = []
    for w, s in enumerate((1, -1)):
        for i, da in enumerate(held):
            slot = spot(da, -s, core)
            fourth.append(send(far_out.at[slot, halves[w]], far_out.at[slot, halves[w]],
                               f_send.at[4 + w, i], f_recv.at[4 + w, i], (spot(0, s, core), me)))
    z_step(3)
    for copy in fourth:
        copy.wait_recv()
    for da in held:
        to_partner(spot(da, 2, core))
    for step in range(4, n - 1):
        z_step(step)
    for way in range(2):
        z_prev[way].wait_recv()
    for copy in partner_copies:
        copy.wait_recv()
    for copy in started:
        copy.wait_send()
    local_own.wait()


def gather_all(own_x, far_x, n, n_far):
    side = 4
    return pl.pallas_call(
        functools.partial(comm_kernel, n, side, own_x.shape[0] // 2, 512),
        out_shape=(
            jax.ShapeDtypeStruct((n,) + own_x.shape, own_x.dtype),
            jax.ShapeDtypeStruct((n_far,) + far_x.shape, far_x.dtype),
        ),
        in_specs=[pl.BlockSpec(memory_space=pl.ANY)] * 2,
        out_specs=(pl.BlockSpec(memory_space=pl.ANY), pl.BlockSpec(memory_space=pl.ANY)),
        scratch_shapes=[
            pltpu.SemaphoreType.DMA((3,)),
            pltpu.SemaphoreType.DMA((2, n - 1)),
            pltpu.SemaphoreType.DMA((2, n - 1)),
            pltpu.SemaphoreType.DMA((6, 4)),
            pltpu.SemaphoreType.DMA((6, 4)),
            pltpu.SemaphoreType.DMA((n_far // 2,)),
            pltpu.SemaphoreType.DMA((n_far // 2,)),
        ],
        compiler_params=pltpu.CompilerParams(collective_id=0, has_side_effects=True),
    )(own_x, far_x)


def split(x):
    hi = x.astype(jnp.bfloat16)
    lo = (x - hi.astype(jnp.float32)).astype(jnp.bfloat16)
    return hi, lo


def dot_t(a, b):
    return lax.dot_general(a, b, (((1,), (1,)), ((), ())), preferred_element_type=jnp.float32)


def normal_kernel(slots, far_per, n_groups, own_meta, far_meta, own_ref, far_ref, out_ref, dense, p_hi, p_lo, x_hi, x_lo, z_hi, z_lo):
    g = pl.program_id(0)

    @pl.when(g == 0)
    def _():
        out_ref[...] = jnp.zeros_like(out_ref)

    dense[...] = jnp.zeros_like(dense)
    own_count = own_meta[(g * 3 + 2) * slots]
    for k in range(slots):

        @pl.when(k < own_count)
        def _():
            r = own_meta[(g * 3 + 0) * slots + k]
            c = own_meta[(g * 3 + 1) * slots + k]
            rows = pl.ds(pl.multiple_of(r * TB, TB), TB)
            cols = pl.ds(pl.multiple_of(c * TB, TB), TB)
            tile = own_ref[0, k * TB : (k + 1) * TB, :]
            dense[rows, cols] += tile * own_ref[0, pl.ds(slots * TB + META + c, 1), :]

    hi, lo = split(dense[...])
    p_hi[...] = hi
    p_lo[...] = lo

    for qi in range(far_per):
        base = (lax.rem(g + 1, n_groups) * far_per + qi) * 3 * slots
        count = far_meta[base + 2 * slots]
        for k in range(slots):
            r = far_meta[base + k]
            c = jnp.minimum(jnp.maximum(far_meta[base + slots + k], 0), CB_DEV - 1)
            src = pl.ds(pl.multiple_of(c * TB, TB), TB)
            x_hi[:, k * TB : (k + 1) * TB] = p_hi[:, src]
            x_lo[:, k * TB : (k + 1) * TB] = p_lo[:, src]
            t_hi, t_lo = split(far_ref[qi, k * TB : (k + 1) * TB, :])
            live = k < count
            for half in range(RB):
                keep = jnp.logical_and(live, r == half)
                z_hi[half * TB : (half + 1) * TB, k * TB : (k + 1) * TB] = jnp.where(keep, t_hi, jnp.zeros_like(t_hi))
                z_lo[half * TB : (half + 1) * TB, k * TB : (k + 1) * TB] = jnp.where(keep, t_lo, jnp.zeros_like(t_lo))
        a_hi = x_hi[...]
        b_hi = z_hi[...]
        prod = dot_t(a_hi, b_hi) + (dot_t(a_hi, z_lo[...]) + dot_t(x_lo[...], b_hi))
        out_ref[:, qi * RB * TB : (qi + 1) * RB * TB] += prod


def per_device(tiles, tile_rows, tile_cols, counts, scaling):
    n_rows = lax.axis_size("rows")
    n_cols = lax.axis_size("cols")
    slots = tiles.shape[1]
    far_per = n_rows // n_cols
    packed = pack(tiles, tile_rows, tile_cols, counts)
    set_len = packed.shape[0]
    own_packed = pack(tiles, tile_rows, tile_cols, counts, scaling)
    own_len = own_packed.shape[0]

    own, far = gather_all(own_packed, packed, n_cols, n_rows)

    own_meta = unpack_meta(own, slots)
    far_meta = unpack_meta(far, slots)
    out_cols = far_per * RB * TB

    grid_spec = pltpu.PrefetchScalarGridSpec(
        num_scalar_prefetch=2,
        grid=(n_cols,),
        in_specs=[
            pl.BlockSpec((1, own_len, TB), lambda g, om, fm: (g, 0, 0)),
            pl.BlockSpec((far_per, set_len, TB), lambda g, om, fm: ((g + 1) % n_cols, 0, 0)),
        ],
        out_specs=pl.BlockSpec((RB * TB, out_cols), lambda g, om, fm: (0, 0)),
        scratch_shapes=[
            pltpu.VMEM((RB * TB, CB_DEV * TB), jnp.float32),
            pltpu.VMEM((RB * TB, CB_DEV * TB), jnp.bfloat16),
            pltpu.VMEM((RB * TB, CB_DEV * TB), jnp.bfloat16),
            pltpu.VMEM((RB * TB, slots * TB), jnp.bfloat16),
            pltpu.VMEM((RB * TB, slots * TB), jnp.bfloat16),
            pltpu.VMEM((RB * TB, slots * TB), jnp.bfloat16),
            pltpu.VMEM((RB * TB, slots * TB), jnp.bfloat16),
        ],
    )
    return pl.pallas_call(
        functools.partial(normal_kernel, slots, far_per, n_cols),
        grid_spec=grid_spec,
        out_shape=jax.ShapeDtypeStruct((RB * TB, out_cols), jnp.float32),
        compiler_params=pltpu.CompilerParams(dimension_semantics=("arbitrary",)),
    )(own_meta, far_meta, own, far)


def solution(mesh):
    placed = (
        P("rows", "cols", None, None),
        P("rows", "cols"),
        P("rows", "cols"),
        P("rows", "cols"),
        P("cols"),
    )
    return jax.shard_map(
        per_device, mesh=mesh, in_specs=placed, out_specs=P("rows", "cols"), check_vma=False
    )
```

```python
import functools

import jax
import jax.numpy as jnp
from jax import lax
from jax.experimental import pallas as pl
from jax.experimental.pallas import tpu as pltpu
from jax.sharding import PartitionSpec as P

TB = 128
RB = 2
CB_DEV = 16
META = 8
MESH = pl.DeviceIdType.MESH


def pack(tiles, tile_rows, tile_cols, counts, scaling=None):
    slots = tiles.shape[1]
    meta = jnp.stack(
        [tile_rows[0], tile_cols[0], jnp.broadcast_to(counts[0, 0], (slots,))]
    ).astype(jnp.float32)
    meta = jnp.pad(meta, ((0, META - 3), (0, TB - slots)))
    parts = [tiles[0].reshape(slots * TB, TB), meta]
    if scaling is not None:
        parts += [scaling.reshape(CB_DEV, TB), jnp.zeros((META, TB), jnp.float32)]
    return jnp.concatenate(parts, axis=0)


def unpack_meta(sets, slots):
    return sets[:, slots * TB : slots * TB + 3, :slots].astype(jnp.int32).reshape(-1)


def comm_kernel(n, side, own_half, far_half, own_x, far_x, own_out, far_out, sems, z_send, z_recv, f_send, f_recv, p_send, p_recv):
    me = lax.axis_index("cols")
    row = lax.axis_index("rows")
    core = row % 2
    y = row // (2 * side)
    x = (row // 2) % side
    step_a = (core, 1 - core)
    step_b = (1 - core, core)

    def spot(da, db, cc):
        yy = (y + da * step_a[0] + db * step_b[0] + 2 * side) % side
        xx = (x + da * step_a[1] + db * step_b[1] + 2 * side) % side
        return (yy * side + xx) * 2 + cc

    z_right = lax.rem(me + 1, n)
    z_left = lax.rem(me + n - 1, n)
    partner = row - core + (1 - core)
    far_per = far_out.shape[0] // n
    dest = (lax.rem(me + 1, n) * far_per + row % far_per, row // far_per)
    origin_plane = lax.rem(row // far_per + n - 1, n)
    source = (me * far_per + row % far_per, origin_plane)
    barrier = pltpu.get_barrier_semaphore()
    peers = [(row, z_left), (row, z_right), (partner, me), dest, source]
    for s in (1, -1):
        peers.append((spot(s, 0, core), me))
        peers.append((spot(0, s, core), me))
    for peer in peers:
        pl.semaphore_signal(barrier, inc=1, device_id=peer, device_id_type=MESH)
    pl.semaphore_wait(barrier, len(peers))

    local_own = pltpu.make_async_copy(own_x, own_out.at[me], sems.at[0])
    local_own.start()

    far_rows = far_x.shape[0]
    halves = (pl.ds(0, far_half), pl.ds(far_half, far_rows - far_half))
    started = []
    partner_copies = []

    def send(src, dst, sem_s, sem_r, peer):
        copy = pltpu.make_async_remote_copy(
            src_ref=src, dst_ref=dst, send_sem=sem_s, recv_sem=sem_r, device_id=peer, device_id_type=MESH
        )
        copy.start()
        started.append(copy)
        return copy

    def to_partner(slot, src=None):
        j = len(partner_copies)
        src = far_out.at[slot] if src is None else src
        partner_copies.append(send(src, far_out.at[slot], p_send.at[j], p_recv.at[j], (partner, me)))

    own_halves = (pl.ds(0, own_half), pl.ds(own_half, own_half))
    z_prev = [None, None]

    def z_step(step):
        if step >= n - 1:
            return
        for way in range(2):
            if way == 0:
                origin = lax.rem(me - step + n, n)
            else:
                origin = lax.rem(me + step, n)
            if step == 0:
                src = own_x.at[own_halves[way]]
            else:
                z_prev[way].wait_recv()
                src = own_out.at[origin, own_halves[way]]
            z_prev[way] = send(
                src, own_out.at[origin, own_halves[way]], z_send.at[way, step], z_recv.at[way, step],
                (row, (z_right, z_left)[way]),
            )

    z_step(0)
    moved = send(far_x, far_out.at[dest[0]], sems.at[1], sems.at[2], dest)
    for step in range(1, 5):
        z_step(step)
    moved.wait_recv()
    to_partner(spot(0, 0, core))
    first = [send(far_out.at[spot(0, 0, core)], far_out.at[spot(0, 0, core)], f_send.at[0, w], f_recv.at[0, w], (spot(s, 0, core), me))
             for w, s in enumerate((1, -1))]
    for copy in first:
        copy.wait_recv()
    to_partner(spot(-1, 0, core))
    to_partner(spot(1, 0, core))
    second = [send(far_out.at[spot(-s, 0, core), halves[w]], far_out.at[spot(-s, 0, core), halves[w]],
                   f_send.at[1, w], f_recv.at[1, w], (spot(s, 0, core), me))
              for w, s in enumerate((1, -1))]
    z_step(5)
    for copy in second:
        copy.wait_recv()
    to_partner(spot(2, 0, core))
    held = (0, -1, 1, 2)
    third = []
    for w, s in enumerate((1, -1)):
        for i, da in enumerate(held):
            slot = spot(da, 0, core)
            third.append(send(far_out.at[slot], far_out.at[slot], f_send.at[2 + w, i], f_recv.at[2 + w, i],
                              (spot(0, s, core), me)))
    z_step(6)
    for copy in third:
        copy.wait_recv()
    for s in (1, -1):
        for da in held:
            to_partner(spot(da, -s, core))
    fourth = []
    for w, s in enumerate((1, -1)):
        for i, da in enumerate(held):
            slot = spot(da, -s, core)
            fourth.append(send(far_out.at[slot, halves[w]], far_out.at[slot, halves[w]],
                               f_send.at[4 + w, i], f_recv.at[4 + w, i], (spot(0, s, core), me)))
    for copy in fourth:
        copy.wait_recv()
    for da in held:
        to_partner(spot(da, 2, core))
    for step in range(7, n - 1):
        z_step(step)
    for way in range(2):
        z_prev[way].wait_recv()
    for copy in partner_copies:
        copy.wait_recv()
    for copy in started:
        copy.wait_send()
    local_own.wait()


def gather_all(own_x, far_x, n, n_far):
    side = 4
    return pl.pallas_call(
        functools.partial(comm_kernel, n, side, own_x.shape[0] // 2, 512),
        out_shape=(
            jax.ShapeDtypeStruct((n,) + own_x.shape, own_x.dtype),
            jax.ShapeDtypeStruct((n_far,) + far_x.shape, far_x.dtype),
        ),
        in_specs=[pl.BlockSpec(memory_space=pl.ANY)] * 2,
        out_specs=(pl.BlockSpec(memory_space=pl.ANY), pl.BlockSpec(memory_space=pl.ANY)),
        scratch_shapes=[
            pltpu.SemaphoreType.DMA((3,)),
            pltpu.SemaphoreType.DMA((2, n - 1)),
            pltpu.SemaphoreType.DMA((2, n - 1)),
            pltpu.SemaphoreType.DMA((6, 4)),
            pltpu.SemaphoreType.DMA((6, 4)),
            pltpu.SemaphoreType.DMA((n_far // 2,)),
            pltpu.SemaphoreType.DMA((n_far // 2,)),
        ],
        compiler_params=pltpu.CompilerParams(collective_id=0, has_side_effects=True),
    )(own_x, far_x)


def split(x):
    hi = x.astype(jnp.bfloat16)
    lo = (x - hi.astype(jnp.float32)).astype(jnp.bfloat16)
    return hi, lo


def dot_t(a, b):
    return lax.dot_general(a, b, (((1,), (1,)), ((), ())), preferred_element_type=jnp.float32)


def normal_kernel(slots, far_per, n_groups, own_meta, far_meta, own_ref, far_ref, out_ref, dense, p_hi, p_lo, x_hi, x_lo, z_hi, z_lo):
    g = pl.program_id(0)

    @pl.when(g == 0)
    def _():
        out_ref[...] = jnp.zeros_like(out_ref)

    dense[...] = jnp.zeros_like(dense)
    own_count = own_meta[(g * 3 + 2) * slots]
    for k in range(slots):

        @pl.when(k < own_count)
        def _():
            r = own_meta[(g * 3 + 0) * slots + k]
            c = own_meta[(g * 3 + 1) * slots + k]
            rows = pl.ds(pl.multiple_of(r * TB, TB), TB)
            cols = pl.ds(pl.multiple_of(c * TB, TB), TB)
            tile = own_ref[0, k * TB : (k + 1) * TB, :]
            dense[rows, cols] += tile * own_ref[0, pl.ds(slots * TB + META + c, 1), :]

    hi, lo = split(dense[...])
    p_hi[...] = hi
    p_lo[...] = lo

    for qi in range(far_per):
        base = (lax.rem(g + 1, n_groups) * far_per + qi) * 3 * slots
        count = far_meta[base + 2 * slots]
        for k in range(slots):
            r = far_meta[base + k]
            c = jnp.minimum(jnp.maximum(far_meta[base + slots + k], 0), CB_DEV - 1)
            src = pl.ds(pl.multiple_of(c * TB, TB), TB)
            x_hi[:, k * TB : (k + 1) * TB] = p_hi[:, src]
            x_lo[:, k * TB : (k + 1) * TB] = p_lo[:, src]
            t_hi, t_lo = split(far_ref[qi, k * TB : (k + 1) * TB, :])
            live = k < count
            for half in range(RB):
                keep = jnp.logical_and(live, r == half)
                z_hi[half * TB : (half + 1) * TB, k * TB : (k + 1) * TB] = jnp.where(keep, t_hi, jnp.zeros_like(t_hi))
                z_lo[half * TB : (half + 1) * TB, k * TB : (k + 1) * TB] = jnp.where(keep, t_lo, jnp.zeros_like(t_lo))
        a_hi = x_hi[...]
        b_hi = z_hi[...]
        prod = dot_t(a_hi, b_hi) + (dot_t(a_hi, z_lo[...]) + dot_t(x_lo[...], b_hi))
        out_ref[:, qi * RB * TB : (qi + 1) * RB * TB] += prod


def per_device(tiles, tile_rows, tile_cols, counts, scaling):
    n_rows = lax.axis_size("rows")
    n_cols = lax.axis_size("cols")
    slots = tiles.shape[1]
    far_per = n_rows // n_cols
    packed = pack(tiles, tile_rows, tile_cols, counts)
    set_len = packed.shape[0]
    own_packed = pack(tiles, tile_rows, tile_cols, counts, scaling)
    own_len = own_packed.shape[0]

    own, far = gather_all(own_packed, packed, n_cols, n_rows)

    own_meta = unpack_meta(own, slots)
    far_meta = unpack_meta(far, slots)
    out_cols = far_per * RB * TB

    grid_spec = pltpu.PrefetchScalarGridSpec(
        num_scalar_prefetch=2,
        grid=(n_cols,),
        in_specs=[
            pl.BlockSpec((1, own_len, TB), lambda g, om, fm: (g, 0, 0)),
            pl.BlockSpec((far_per, set_len, TB), lambda g, om, fm: ((g + 1) % n_cols, 0, 0)),
        ],
        out_specs=pl.BlockSpec((RB * TB, out_cols), lambda g, om, fm: (0, 0)),
        scratch_shapes=[
            pltpu.VMEM((RB * TB, CB_DEV * TB), jnp.float32),
            pltpu.VMEM((RB * TB, CB_DEV * TB), jnp.bfloat16),
            pltpu.VMEM((RB * TB, CB_DEV * TB), jnp.bfloat16),
            pltpu.VMEM((RB * TB, slots * TB), jnp.bfloat16),
            pltpu.VMEM((RB * TB, slots * TB), jnp.bfloat16),
            pltpu.VMEM((RB * TB, slots * TB), jnp.bfloat16),
            pltpu.VMEM((RB * TB, slots * TB), jnp.bfloat16),
        ],
    )
    return pl.pallas_call(
        functools.partial(normal_kernel, slots, far_per, n_cols),
        grid_spec=grid_spec,
        out_shape=jax.ShapeDtypeStruct((RB * TB, out_cols), jnp.float32),
        compiler_params=pltpu.CompilerParams(dimension_semantics=("arbitrary",)),
    )(own_meta, far_meta, own, far)


def solution(mesh):
    placed = (
        P("rows", "cols", None, None),
        P("rows", "cols"),
        P("rows", "cols"),
        P("rows", "cols"),
        P("cols"),
    )
    return jax.shard_map(
        per_device, mesh=mesh, in_specs=placed, out_specs=P("rows", "cols"), check_vma=False
    )
```

```python
import functools

import jax
import jax.numpy as jnp
from jax import lax
from jax.experimental import pallas as pl
from jax.experimental.pallas import tpu as pltpu
from jax.sharding import PartitionSpec as P

TB = 128
RB = 2
CB_DEV = 16
META = 8
MESH = pl.DeviceIdType.MESH


def pack(tiles, tile_rows, tile_cols, counts, scaling=None):
    slots = tiles.shape[1]
    meta = jnp.stack(
        [tile_rows[0], tile_cols[0], jnp.broadcast_to(counts[0, 0], (slots,))]
    ).astype(jnp.float32)
    meta = jnp.pad(meta, ((0, META - 3), (0, TB - slots)))
    parts = [tiles[0].reshape(slots * TB, TB), meta]
    if scaling is not None:
        parts += [scaling.reshape(CB_DEV, TB), jnp.zeros((META, TB), jnp.float32)]
    return jnp.concatenate(parts, axis=0)


def unpack_meta(sets, slots):
    return sets[:, slots * TB : slots * TB + 3, :slots].astype(jnp.int32).reshape(-1)


def comm_kernel(n, side, own_half, far_half, own_x, far_x, own_out, far_out, sems, perm_send, perm_recv, z_send, z_recv, f_send, f_recv, p_send, p_recv):
    me = lax.axis_index("cols")
    row = lax.axis_index("rows")
    core = row % 2
    y = row // (2 * side)
    x = (row // 2) % side
    step_a = (core, 1 - core)
    step_b = (1 - core, core)

    def spot(da, db, cc):
        yy = (y + da * step_a[0] + db * step_b[0] + 2 * side) % side
        xx = (x + da * step_a[1] + db * step_b[1] + 2 * side) % side
        return (yy * side + xx) * 2 + cc

    z_right = lax.rem(me + 1, n)
    z_left = lax.rem(me + n - 1, n)
    partner = row - core + (1 - core)
    far_per = far_out.shape[0] // n
    dest = (lax.rem(me + 1, n) * far_per + row % far_per, row // far_per)
    origin_plane = lax.rem(row // far_per + n - 1, n)
    source = (me * far_per + row % far_per, origin_plane)
    barrier = pltpu.get_barrier_semaphore()
    peers = [(row, z_left), (row, z_right), (partner, me), dest, source]
    for s in (1, -1):
        peers.append((spot(s, 0, core), me))
        peers.append((spot(0, s, core), me))
    for peer in peers:
        pl.semaphore_signal(barrier, inc=1, device_id=peer, device_id_type=MESH)
    pl.semaphore_wait(barrier, len(peers))

    local_own = pltpu.make_async_copy(own_x, own_out.at[me], sems.at[0])
    local_own.start()

    far_rows = far_x.shape[0]
    cut = far_half
    chunks = (pl.ds(0, cut), pl.ds(cut, far_rows - cut))
    first_half = (cut // 2) // META * META
    second_half = ((far_rows - cut) // 2) // META * META
    halves = (
        (pl.ds(0, first_half), pl.ds(first_half, cut - first_half)),
        (pl.ds(cut, second_half), pl.ds(cut + second_half, far_rows - cut - second_half)),
    )
    started = []
    partner_count = [0, 0]
    partner_copies = []

    def send(src, dst, sem_s, sem_r, peer):
        copy = pltpu.make_async_remote_copy(
            src_ref=src, dst_ref=dst, send_sem=sem_s, recv_sem=sem_r, device_id=peer, device_id_type=MESH
        )
        copy.start()
        started.append(copy)
        return copy

    def to_partner(h, slot):
        j = partner_count[h]
        partner_count[h] += 1
        ref = far_out.at[slot, chunks[h]]
        partner_copies.append(send(ref, ref, p_send.at[h, j], p_recv.at[h, j], (partner, me)))

    own_halves = (pl.ds(0, own_half), pl.ds(own_half, own_half))
    z_prev = [None, None]

    def z_step(step):
        if step >= n - 1:
            return
        for way in range(2):
            if way == 0:
                origin = lax.rem(me - step + n, n)
            else:
                origin = lax.rem(me + step, n)
            if step == 0:
                src = own_x.at[own_halves[way]]
            else:
                z_prev[way].wait_recv()
                src = own_out.at[origin, own_halves[way]]
            z_prev[way] = send(
                src, own_out.at[origin, own_halves[way]], z_send.at[way, step], z_recv.at[way, step],
                (row, (z_right, z_left)[way]),
            )

    held = (0, -1, 1, 2)

    def far_stages(h):
        box = {}
        rows = chunks[h]

        def s0():
            box["moved"] = send(far_x.at[rows], far_out.at[dest[0], rows], perm_send.at[h], perm_recv.at[h], dest)

        def s1():
            box["moved"].wait_recv()
            to_partner(h, spot(0, 0, core))
            box["first"] = [
                send(far_out.at[spot(0, 0, core), rows], far_out.at[spot(0, 0, core), rows],
                     f_send.at[h, 0, w], f_recv.at[h, 0, w], (spot(s, 0, core), me))
                for w, s in enumerate((1, -1))
            ]

        def s2():
            for copy in box["first"]:
                copy.wait_recv()
            to_partner(h, spot(-1, 0, core))
            to_partner(h, spot(1, 0, core))
            box["second"] = [
                send(far_out.at[spot(-s, 0, core), halves[h][w]], far_out.at[spot(-s, 0, core), halves[h][w]],
                     f_send.at[h, 1, w], f_recv.at[h, 1, w], (spot(s, 0, core), me))
                for w, s in enumerate((1, -1))
            ]

        def s3():
            for copy in box["second"]:
                copy.wait_recv()
            to_partner(h, spot(2, 0, core))
            box["third"] = []
            for w, s in enumerate((1, -1)):
                for i, da in enumerate(held):
                    slot = spot(da, 0, core)
                    box["third"].append(send(far_out.at[slot, rows], far_out.at[slot, rows],
                                             f_send.at[h, 2 + w, i], f_recv.at[h, 2 + w, i], (spot(0, s, core), me)))

        def s4():
            for copy in box["third"]:
                copy.wait_recv()
            for s in (1, -1):
                for da in held:
                    to_partner(h, spot(da, -s, core))
            box["fourth"] = []
            for w, s in enumerate((1, -1)):
                for i, da in enumerate(held):
                    slot = spot(da, -s, core)
                    box["fourth"].append(send(far_out.at[slot, halves[h][w]], far_out.at[slot, halves[h][w]],
                                              f_send.at[h, 4 + w, i], f_recv.at[h, 4 + w, i], (spot(0, s, core), me)))

        def s5():
            for copy in box["fourth"]:
                copy.wait_recv()
            for da in held:
                to_partner(h, spot(da, 2, core))

        return [s0, s1, s2, s3, s4, s5]

    lead = far_stages(0)
    lag = far_stages(1)
    z_step(0)
    lead[0]()
    for tick in range(1, len(lead) + 1):
        if tick < len(lead):
            lead[tick]()
        lag[tick - 1]()
        z_step(tick)
    for step in range(len(lead) + 1, n - 1):
        z_step(step)
    for way in range(2):
        z_prev[way].wait_recv()
    for copy in partner_copies:
        copy.wait_recv()
    for copy in started:
        copy.wait_send()
    local_own.wait()


def gather_all(own_x, far_x, n, n_far):
    side = 4
    return pl.pallas_call(
        functools.partial(comm_kernel, n, side, own_x.shape[0] // 2, 512),
        out_shape=(
            jax.ShapeDtypeStruct((n,) + own_x.shape, own_x.dtype),
            jax.ShapeDtypeStruct((n_far,) + far_x.shape, far_x.dtype),
        ),
        in_specs=[pl.BlockSpec(memory_space=pl.ANY)] * 2,
        out_specs=(pl.BlockSpec(memory_space=pl.ANY), pl.BlockSpec(memory_space=pl.ANY)),
        scratch_shapes=[
            pltpu.SemaphoreType.DMA((1,)),
            pltpu.SemaphoreType.DMA((2,)),
            pltpu.SemaphoreType.DMA((2,)),
            pltpu.SemaphoreType.DMA((2, n - 1)),
            pltpu.SemaphoreType.DMA((2, n - 1)),
            pltpu.SemaphoreType.DMA((2, 6, 4)),
            pltpu.SemaphoreType.DMA((2, 6, 4)),
            pltpu.SemaphoreType.DMA((2, n_far // 2)),
            pltpu.SemaphoreType.DMA((2, n_far // 2)),
        ],
        compiler_params=pltpu.CompilerParams(collective_id=0, has_side_effects=True),
    )(own_x, far_x)


def split(x):
    hi = x.astype(jnp.bfloat16)
    lo = (x - hi.astype(jnp.float32)).astype(jnp.bfloat16)
    return hi, lo


def dot_t(a, b):
    return lax.dot_general(a, b, (((1,), (1,)), ((), ())), preferred_element_type=jnp.float32)


def normal_kernel(slots, far_per, n_groups, own_meta, far_meta, own_ref, far_ref, out_ref, dense, p_hi, p_lo, x_hi, x_lo, z_hi, z_lo):
    g = pl.program_id(0)

    @pl.when(g == 0)
    def _():
        out_ref[...] = jnp.zeros_like(out_ref)

    dense[...] = jnp.zeros_like(dense)
    own_count = own_meta[(g * 3 + 2) * slots]
    for k in range(slots):

        @pl.when(k < own_count)
        def _():
            r = own_meta[(g * 3 + 0) * slots + k]
            c = own_meta[(g * 3 + 1) * slots + k]
            rows = pl.ds(pl.multiple_of(r * TB, TB), TB)
            cols = pl.ds(pl.multiple_of(c * TB, TB), TB)
            tile = own_ref[0, k * TB : (k + 1) * TB, :]
            dense[rows, cols] += tile * own_ref[0, pl.ds(slots * TB + META + c, 1), :]

    hi, lo = split(dense[...])
    p_hi[...] = hi
    p_lo[...] = lo

    for qi in range(far_per):
        base = (lax.rem(g + 1, n_groups) * far_per + qi) * 3 * slots
        count = far_meta[base + 2 * slots]
        for k in range(slots):
            r = far_meta[base + k]
            c = jnp.minimum(jnp.maximum(far_meta[base + slots + k], 0), CB_DEV - 1)
            src = pl.ds(pl.multiple_of(c * TB, TB), TB)
            x_hi[:, k * TB : (k + 1) * TB] = p_hi[:, src]
            x_lo[:, k * TB : (k + 1) * TB] = p_lo[:, src]
            t_hi, t_lo = split(far_ref[qi, k * TB : (k + 1) * TB, :])
            live = k < count
            for half in range(RB):
                keep = jnp.logical_and(live, r == half)
                z_hi[half * TB : (half + 1) * TB, k * TB : (k + 1) * TB] = jnp.where(keep, t_hi, jnp.zeros_like(t_hi))
                z_lo[half * TB : (half + 1) * TB, k * TB : (k + 1) * TB] = jnp.where(keep, t_lo, jnp.zeros_like(t_lo))
        a_hi = x_hi[...]
        b_hi = z_hi[...]
        prod = dot_t(a_hi, b_hi) + (dot_t(a_hi, z_lo[...]) + dot_t(x_lo[...], b_hi))
        out_ref[:, qi * RB * TB : (qi + 1) * RB * TB] += prod


def per_device(tiles, tile_rows, tile_cols, counts, scaling):
    n_rows = lax.axis_size("rows")
    n_cols = lax.axis_size("cols")
    slots = tiles.shape[1]
    far_per = n_rows // n_cols
    packed = pack(tiles, tile_rows, tile_cols, counts)
    set_len = packed.shape[0]
    own_packed = pack(tiles, tile_rows, tile_cols, counts, scaling)
    own_len = own_packed.shape[0]

    own, far = gather_all(own_packed, packed, n_cols, n_rows)

    own_meta = unpack_meta(own, slots)
    far_meta = unpack_meta(far, slots)
    out_cols = far_per * RB * TB

    grid_spec = pltpu.PrefetchScalarGridSpec(
        num_scalar_prefetch=2,
        grid=(n_cols,),
        in_specs=[
            pl.BlockSpec((1, own_len, TB), lambda g, om, fm: (g, 0, 0)),
            pl.BlockSpec((far_per, set_len, TB), lambda g, om, fm: ((g + 1) % n_cols, 0, 0)),
        ],
        out_specs=pl.BlockSpec((RB * TB, out_cols), lambda g, om, fm: (0, 0)),
        scratch_shapes=[
            pltpu.VMEM((RB * TB, CB_DEV * TB), jnp.float32),
            pltpu.VMEM((RB * TB, CB_DEV * TB), jnp.bfloat16),
            pltpu.VMEM((RB * TB, CB_DEV * TB), jnp.bfloat16),
            pltpu.VMEM((RB * TB, slots * TB), jnp.bfloat16),
            pltpu.VMEM((RB * TB, slots * TB), jnp.bfloat16),
            pltpu.VMEM((RB * TB, slots * TB), jnp.bfloat16),
            pltpu.VMEM((RB * TB, slots * TB), jnp.bfloat16),
        ],
    )
    return pl.pallas_call(
        functools.partial(normal_kernel, slots, far_per, n_cols),
        grid_spec=grid_spec,
        out_shape=jax.ShapeDtypeStruct((RB * TB, out_cols), jnp.float32),
        compiler_params=pltpu.CompilerParams(dimension_semantics=("arbitrary",)),
    )(own_meta, far_meta, own, far)


def solution(mesh):
    placed = (
        P("rows", "cols", None, None),
        P("rows", "cols"),
        P("rows", "cols"),
        P("rows", "cols"),
        P("cols"),
    )
    return jax.shard_map(
        per_device, mesh=mesh, in_specs=placed, out_specs=P("rows", "cols"), check_vma=False
    )
```

```python
import functools

import jax
import jax.numpy as jnp
from jax import lax
from jax.experimental import pallas as pl
from jax.experimental.pallas import tpu as pltpu
from jax.sharding import PartitionSpec as P

TB = 128
RB = 2
CB_DEV = 16
META = 8
MESH = pl.DeviceIdType.MESH
CHUNKS = 4


def pack(tiles, tile_rows, tile_cols, counts, scaling=None):
    slots = tiles.shape[1]
    meta = jnp.stack(
        [tile_rows[0], tile_cols[0], jnp.broadcast_to(counts[0, 0], (slots,))]
    ).astype(jnp.float32)
    meta = jnp.pad(meta, ((0, META - 3), (0, TB - slots)))
    parts = [tiles[0].reshape(slots * TB, TB), meta]
    if scaling is not None:
        parts += [scaling.reshape(CB_DEV, TB), jnp.zeros((META, TB), jnp.float32)]
    return jnp.concatenate(parts, axis=0)


def unpack_meta(sets, slots):
    return sets[:, slots * TB : slots * TB + 3, :slots].astype(jnp.int32).reshape(-1)


def comm_kernel(n, side, own_half, n_chunks, own_x, far_x, own_out, far_out, sems, perm_send, perm_recv, z_send, z_recv, f_send, f_recv, p_send, p_recv):
    me = lax.axis_index("cols")
    row = lax.axis_index("rows")
    core = row % 2
    y = row // (2 * side)
    x = (row // 2) % side
    step_a = (core, 1 - core)
    step_b = (1 - core, core)

    def spot(da, db, cc):
        yy = (y + da * step_a[0] + db * step_b[0] + 2 * side) % side
        xx = (x + da * step_a[1] + db * step_b[1] + 2 * side) % side
        return (yy * side + xx) * 2 + cc

    z_right = lax.rem(me + 1, n)
    z_left = lax.rem(me + n - 1, n)
    partner = row - core + (1 - core)
    far_per = far_out.shape[0] // n
    dest = (lax.rem(me + 1, n) * far_per + row % far_per, row // far_per)
    origin_plane = lax.rem(row // far_per + n - 1, n)
    source = (me * far_per + row % far_per, origin_plane)
    barrier = pltpu.get_barrier_semaphore()
    peers = [(row, z_left), (row, z_right), (partner, me), dest, source]
    for s in (1, -1):
        peers.append((spot(s, 0, core), me))
        peers.append((spot(0, s, core), me))
    for peer in peers:
        pl.semaphore_signal(barrier, inc=1, device_id=peer, device_id_type=MESH)
    pl.semaphore_wait(barrier, len(peers))

    local_own = pltpu.make_async_copy(own_x, own_out.at[me], sems.at[0])
    local_own.start()

    far_rows = far_x.shape[0]
    size = (far_rows // n_chunks) // META * META
    bounds = [h * size for h in range(n_chunks)] + [far_rows]
    chunks = []
    halves = []
    for h in range(n_chunks):
        low, high = bounds[h], bounds[h + 1]
        mid = low + ((high - low) // 2) // META * META
        chunks.append(pl.ds(low, high - low))
        halves.append((pl.ds(low, mid - low), pl.ds(mid, high - mid)))
    started = []
    partner_count = [0] * n_chunks
    partner_copies = []

    def send(src, dst, sem_s, sem_r, peer):
        copy = pltpu.make_async_remote_copy(
            src_ref=src, dst_ref=dst, send_sem=sem_s, recv_sem=sem_r, device_id=peer, device_id_type=MESH
        )
        copy.start()
        started.append(copy)
        return copy

    def to_partner(h, slot):
        j = partner_count[h]
        partner_count[h] += 1
        ref = far_out.at[slot, chunks[h]]
        partner_copies.append(send(ref, ref, p_send.at[h, j], p_recv.at[h, j], (partner, me)))

    own_halves = (pl.ds(0, own_half), pl.ds(own_half, own_half))
    z_prev = [None, None]

    def z_step(step):
        if step >= n - 1:
            return
        for way in range(2):
            if way == 0:
                origin = lax.rem(me - step + n, n)
            else:
                origin = lax.rem(me + step, n)
            if step == 0:
                src = own_x.at[own_halves[way]]
            else:
                z_prev[way].wait_recv()
                src = own_out.at[origin, own_halves[way]]
            z_prev[way] = send(
                src, own_out.at[origin, own_halves[way]], z_send.at[way, step], z_recv.at[way, step],
                (row, (z_right, z_left)[way]),
            )

    held = (0, -1, 1, 2)

    def far_stages(h):
        box = {}
        rows = chunks[h]

        def s0():
            box["moved"] = send(far_x.at[rows], far_out.at[dest[0], rows], perm_send.at[h], perm_recv.at[h], dest)

        def s1():
            box["moved"].wait_recv()
            to_partner(h, spot(0, 0, core))
            box["first"] = [
                send(far_out.at[spot(0, 0, core), rows], far_out.at[spot(0, 0, core), rows],
                     f_send.at[h, 0, w], f_recv.at[h, 0, w], (spot(s, 0, core), me))
                for w, s in enumerate((1, -1))
            ]

        def s2():
            for copy in box["first"]:
                copy.wait_recv()
            to_partner(h, spot(-1, 0, core))
            to_partner(h, spot(1, 0, core))
            box["second"] = [
                send(far_out.at[spot(-s, 0, core), halves[h][w]], far_out.at[spot(-s, 0, core), halves[h][w]],
                     f_send.at[h, 1, w], f_recv.at[h, 1, w], (spot(s, 0, core), me))
                for w, s in enumerate((1, -1))
            ]

        def s3():
            for copy in box["second"]:
                copy.wait_recv()
            to_partner(h, spot(2, 0, core))
            box["third"] = []
            for w, s in enumerate((1, -1)):
                for i, da in enumerate(held):
                    slot = spot(da, 0, core)
                    box["third"].append(send(far_out.at[slot, rows], far_out.at[slot, rows],
                                             f_send.at[h, 2 + w, i], f_recv.at[h, 2 + w, i], (spot(0, s, core), me)))

        def s4():
            for copy in box["third"]:
                copy.wait_recv()
            for s in (1, -1):
                for da in held:
                    to_partner(h, spot(da, -s, core))
            box["fourth"] = []
            for w, s in enumerate((1, -1)):
                for i, da in enumerate(held):
                    slot = spot(da, -s, core)
                    box["fourth"].append(send(far_out.at[slot, halves[h][w]], far_out.at[slot, halves[h][w]],
                                              f_send.at[h, 4 + w, i], f_recv.at[h, 4 + w, i], (spot(0, s, core), me)))

        def s5():
            for copy in box["fourth"]:
                copy.wait_recv()
            for da in held:
                to_partner(h, spot(da, 2, core))

        return [s0, s1, s2, s3, s4, s5]

    streams = [far_stages(h) for h in range(n_chunks)]
    depth = len(streams[0])
    ticks = depth + n_chunks - 1
    for tick in range(ticks):
        for h in range(n_chunks):
            if 0 <= tick - h < depth:
                streams[h][tick - h]()
        z_step(tick)
    for step in range(ticks, n - 1):
        z_step(step)
    for way in range(2):
        z_prev[way].wait_recv()
    for copy in partner_copies:
        copy.wait_recv()
    for copy in started:
        copy.wait_send()
    local_own.wait()


def gather_all(own_x, far_x, n, n_far):
    side = 4
    return pl.pallas_call(
        functools.partial(comm_kernel, n, side, own_x.shape[0] // 2, CHUNKS),
        out_shape=(
            jax.ShapeDtypeStruct((n,) + own_x.shape, own_x.dtype),
            jax.ShapeDtypeStruct((n_far,) + far_x.shape, far_x.dtype),
        ),
        in_specs=[pl.BlockSpec(memory_space=pl.ANY)] * 2,
        out_specs=(pl.BlockSpec(memory_space=pl.ANY), pl.BlockSpec(memory_space=pl.ANY)),
        scratch_shapes=[
            pltpu.SemaphoreType.DMA((1,)),
            pltpu.SemaphoreType.DMA((CHUNKS,)),
            pltpu.SemaphoreType.DMA((CHUNKS,)),
            pltpu.SemaphoreType.DMA((2, n - 1)),
            pltpu.SemaphoreType.DMA((2, n - 1)),
            pltpu.SemaphoreType.DMA((CHUNKS, 6, 4)),
            pltpu.SemaphoreType.DMA((CHUNKS, 6, 4)),
            pltpu.SemaphoreType.DMA((CHUNKS, n_far // 2)),
            pltpu.SemaphoreType.DMA((CHUNKS, n_far // 2)),
        ],
        compiler_params=pltpu.CompilerParams(collective_id=0, has_side_effects=True),
    )(own_x, far_x)


def split(x):
    hi = x.astype(jnp.bfloat16)
    lo = (x - hi.astype(jnp.float32)).astype(jnp.bfloat16)
    return hi, lo


def dot_t(a, b):
    return lax.dot_general(a, b, (((1,), (1,)), ((), ())), preferred_element_type=jnp.float32)


def normal_kernel(slots, far_per, n_groups, own_meta, far_meta, own_ref, far_ref, out_ref, dense, p_hi, p_lo, x_hi, x_lo, z_hi, z_lo):
    g = pl.program_id(0)

    @pl.when(g == 0)
    def _():
        out_ref[...] = jnp.zeros_like(out_ref)

    dense[...] = jnp.zeros_like(dense)
    own_count = own_meta[(g * 3 + 2) * slots]
    for k in range(slots):

        @pl.when(k < own_count)
        def _():
            r = own_meta[(g * 3 + 0) * slots + k]
            c = own_meta[(g * 3 + 1) * slots + k]
            rows = pl.ds(pl.multiple_of(r * TB, TB), TB)
            cols = pl.ds(pl.multiple_of(c * TB, TB), TB)
            tile = own_ref[0, k * TB : (k + 1) * TB, :]
            dense[rows, cols] += tile * own_ref[0, pl.ds(slots * TB + META + c, 1), :]

    hi, lo = split(dense[...])
    p_hi[...] = hi
    p_lo[...] = lo

    for qi in range(far_per):
        base = (lax.rem(g + 1, n_groups) * far_per + qi) * 3 * slots
        count = far_meta[base + 2 * slots]
        for k in range(slots):
            r = far_meta[base + k]
            c = jnp.minimum(jnp.maximum(far_meta[base + slots + k], 0), CB_DEV - 1)
            src = pl.ds(pl.multiple_of(c * TB, TB), TB)
            x_hi[:, k * TB : (k + 1) * TB] = p_hi[:, src]
            x_lo[:, k * TB : (k + 1) * TB] = p_lo[:, src]
            t_hi, t_lo = split(far_ref[qi, k * TB : (k + 1) * TB, :])
            live = k < count
            for half in range(RB):
                keep = jnp.logical_and(live, r == half)
                z_hi[half * TB : (half + 1) * TB, k * TB : (k + 1) * TB] = jnp.where(keep, t_hi, jnp.zeros_like(t_hi))
                z_lo[half * TB : (half + 1) * TB, k * TB : (k + 1) * TB] = jnp.where(keep, t_lo, jnp.zeros_like(t_lo))
        a_hi = x_hi[...]
        b_hi = z_hi[...]
        prod = dot_t(a_hi, b_hi) + (dot_t(a_hi, z_lo[...]) + dot_t(x_lo[...], b_hi))
        out_ref[:, qi * RB * TB : (qi + 1) * RB * TB] += prod


def per_device(tiles, tile_rows, tile_cols, counts, scaling):
    n_rows = lax.axis_size("rows")
    n_cols = lax.axis_size("cols")
    slots = tiles.shape[1]
    far_per = n_rows // n_cols
    packed = pack(tiles, tile_rows, tile_cols, counts)
    set_len = packed.shape[0]
    own_packed = pack(tiles, tile_rows, tile_cols, counts, scaling)
    own_len = own_packed.shape[0]

    own, far = gather_all(own_packed, packed, n_cols, n_rows)

    own_meta = unpack_meta(own, slots)
    far_meta = unpack_meta(far, slots)
    out_cols = far_per * RB * TB

    grid_spec = pltpu.PrefetchScalarGridSpec(
        num_scalar_prefetch=2,
        grid=(n_cols,),
        in_specs=[
            pl.BlockSpec((1, own_len, TB), lambda g, om, fm: (g, 0, 0)),
            pl.BlockSpec((far_per, set_len, TB), lambda g, om, fm: ((g + 1) % n_cols, 0, 0)),
        ],
        out_specs=pl.BlockSpec((RB * TB, out_cols), lambda g, om, fm: (0, 0)),
        scratch_shapes=[
            pltpu.VMEM((RB * TB, CB_DEV * TB), jnp.float32),
            pltpu.VMEM((RB * TB, CB_DEV * TB), jnp.bfloat16),
            pltpu.VMEM((RB * TB, CB_DEV * TB), jnp.bfloat16),
            pltpu.VMEM((RB * TB, slots * TB), jnp.bfloat16),
            pltpu.VMEM((RB * TB, slots * TB), jnp.bfloat16),
            pltpu.VMEM((RB * TB, slots * TB), jnp.bfloat16),
            pltpu.VMEM((RB * TB, slots * TB), jnp.bfloat16),
        ],
    )
    return pl.pallas_call(
        functools.partial(normal_kernel, slots, far_per, n_cols),
        grid_spec=grid_spec,
        out_shape=jax.ShapeDtypeStruct((RB * TB, out_cols), jnp.float32),
        compiler_params=pltpu.CompilerParams(dimension_semantics=("arbitrary",)),
    )(own_meta, far_meta, own, far)


def solution(mesh):
    placed = (
        P("rows", "cols", None, None),
        P("rows", "cols"),
        P("rows", "cols"),
        P("rows", "cols"),
        P("cols"),
    )
    return jax.shard_map(
        per_device, mesh=mesh, in_specs=placed, out_specs=P("rows", "cols"), check_vma=False
    )
```

```python
import functools

import jax
import jax.numpy as jnp
from jax import lax
from jax.experimental import pallas as pl
from jax.experimental.pallas import tpu as pltpu
from jax.sharding import PartitionSpec as P

TB = 128
RB = 2
CB_DEV = 16
META = 8
MESH = pl.DeviceIdType.MESH
CHUNKS = 8


def pack(tiles, tile_rows, tile_cols, counts, scaling=None):
    slots = tiles.shape[1]
    meta = jnp.stack(
        [tile_rows[0], tile_cols[0], jnp.broadcast_to(counts[0, 0], (slots,))]
    ).astype(jnp.float32)
    meta = jnp.pad(meta, ((0, META - 3), (0, TB - slots)))
    parts = [tiles[0].reshape(slots * TB, TB), meta]
    if scaling is not None:
        parts += [scaling.reshape(CB_DEV, TB), jnp.zeros((META, TB), jnp.float32)]
    return jnp.concatenate(parts, axis=0)


def unpack_meta(sets, slots):
    return sets[:, slots * TB : slots * TB + 3, :slots].astype(jnp.int32).reshape(-1)


def comm_kernel(n, side, own_half, n_chunks, own_x, far_x, own_out, far_out, sems, perm_send, perm_recv, z_send, z_recv, f_send, f_recv, p_send, p_recv):
    me = lax.axis_index("cols")
    row = lax.axis_index("rows")
    core = row % 2
    y = row // (2 * side)
    x = (row // 2) % side
    step_a = (core, 1 - core)
    step_b = (1 - core, core)

    def spot(da, db, cc):
        yy = (y + da * step_a[0] + db * step_b[0] + 2 * side) % side
        xx = (x + da * step_a[1] + db * step_b[1] + 2 * side) % side
        return (yy * side + xx) * 2 + cc

    z_right = lax.rem(me + 1, n)
    z_left = lax.rem(me + n - 1, n)
    partner = row - core + (1 - core)
    far_per = far_out.shape[0] // n
    dest = (lax.rem(me + 1, n) * far_per + row % far_per, row // far_per)
    origin_plane = lax.rem(row // far_per + n - 1, n)
    source = (me * far_per + row % far_per, origin_plane)
    barrier = pltpu.get_barrier_semaphore()
    peers = [(row, z_left), (row, z_right), (partner, me), dest, source]
    for s in (1, -1):
        peers.append((spot(s, 0, core), me))
        peers.append((spot(0, s, core), me))
    for peer in peers:
        pl.semaphore_signal(barrier, inc=1, device_id=peer, device_id_type=MESH)
    pl.semaphore_wait(barrier, len(peers))

    local_own = pltpu.make_async_copy(own_x, own_out.at[me], sems.at[0])
    local_own.start()

    far_rows = far_x.shape[0]
    size = (far_rows // n_chunks) // META * META
    bounds = [h * size for h in range(n_chunks)] + [far_rows]
    chunks = []
    halves = []
    for h in range(n_chunks):
        low, high = bounds[h], bounds[h + 1]
        mid = low + ((high - low) // 2) // META * META
        chunks.append(pl.ds(low, high - low))
        halves.append((pl.ds(low, mid - low), pl.ds(mid, high - mid)))
    started = []
    partner_count = [0] * n_chunks
    partner_copies = []

    def send(src, dst, sem_s, sem_r, peer):
        copy = pltpu.make_async_remote_copy(
            src_ref=src, dst_ref=dst, send_sem=sem_s, recv_sem=sem_r, device_id=peer, device_id_type=MESH
        )
        copy.start()
        started.append(copy)
        return copy

    def to_partner(h, slot):
        j = partner_count[h]
        partner_count[h] += 1
        ref = far_out.at[slot, chunks[h]]
        partner_copies.append(send(ref, ref, p_send.at[h, j], p_recv.at[h, j], (partner, me)))

    own_halves = (pl.ds(0, own_half), pl.ds(own_half, own_half))
    z_prev = [None, None]

    def z_step(step):
        if step >= n - 1:
            return
        for way in range(2):
            if way == 0:
                origin = lax.rem(me - step + n, n)
            else:
                origin = lax.rem(me + step, n)
            if step == 0:
                src = own_x.at[own_halves[way]]
            else:
                z_prev[way].wait_recv()
                src = own_out.at[origin, own_halves[way]]
            z_prev[way] = send(
                src, own_out.at[origin, own_halves[way]], z_send.at[way, step], z_recv.at[way, step],
                (row, (z_right, z_left)[way]),
            )

    held = (0, -1, 1, 2)

    def far_stages(h):
        box = {}
        rows = chunks[h]

        def s0():
            box["moved"] = send(far_x.at[rows], far_out.at[dest[0], rows], perm_send.at[h], perm_recv.at[h], dest)

        def s1():
            box["moved"].wait_recv()
            to_partner(h, spot(0, 0, core))
            box["first"] = [
                send(far_out.at[spot(0, 0, core), rows], far_out.at[spot(0, 0, core), rows],
                     f_send.at[h, 0, w], f_recv.at[h, 0, w], (spot(s, 0, core), me))
                for w, s in enumerate((1, -1))
            ]

        def s2():
            for copy in box["first"]:
                copy.wait_recv()
            to_partner(h, spot(-1, 0, core))
            to_partner(h, spot(1, 0, core))
            box["second"] = [
                send(far_out.at[spot(-s, 0, core), halves[h][w]], far_out.at[spot(-s, 0, core), halves[h][w]],
                     f_send.at[h, 1, w], f_recv.at[h, 1, w], (spot(s, 0, core), me))
                for w, s in enumerate((1, -1))
            ]

        def s3():
            for copy in box["second"]:
                copy.wait_recv()
            to_partner(h, spot(2, 0, core))
            box["third"] = []
            for w, s in enumerate((1, -1)):
                for i, da in enumerate(held):
                    slot = spot(da, 0, core)
                    box["third"].append(send(far_out.at[slot, rows], far_out.at[slot, rows],
                                             f_send.at[h, 2 + w, i], f_recv.at[h, 2 + w, i], (spot(0, s, core), me)))

        def s4():
            for copy in box["third"]:
                copy.wait_recv()
            for s in (1, -1):
                for da in held:
                    to_partner(h, spot(da, -s, core))
            box["fourth"] = []
            for w, s in enumerate((1, -1)):
                for i, da in enumerate(held):
                    slot = spot(da, -s, core)
                    box["fourth"].append(send(far_out.at[slot, halves[h][w]], far_out.at[slot, halves[h][w]],
                                              f_send.at[h, 4 + w, i], f_recv.at[h, 4 + w, i], (spot(0, s, core), me)))

        def s5():
            for copy in box["fourth"]:
                copy.wait_recv()
            for da in held:
                to_partner(h, spot(da, 2, core))

        return [s0, s1, s2, s3, s4, s5]

    streams = [far_stages(h) for h in range(n_chunks)]
    depth = len(streams[0])
    ticks = depth + n_chunks - 1
    for tick in range(ticks):
        for h in range(n_chunks):
            if 0 <= tick - h < depth:
                streams[h][tick - h]()
        z_step(tick)
    for step in range(ticks, n - 1):
        z_step(step)
    for way in range(2):
        z_prev[way].wait_recv()
    for copy in partner_copies:
        copy.wait_recv()
    for copy in started:
        copy.wait_send()
    local_own.wait()


def gather_all(own_x, far_x, n, n_far):
    side = 4
    return pl.pallas_call(
        functools.partial(comm_kernel, n, side, own_x.shape[0] // 2, CHUNKS),
        out_shape=(
            jax.ShapeDtypeStruct((n,) + own_x.shape, own_x.dtype),
            jax.ShapeDtypeStruct((n_far,) + far_x.shape, far_x.dtype),
        ),
        in_specs=[pl.BlockSpec(memory_space=pl.ANY)] * 2,
        out_specs=(pl.BlockSpec(memory_space=pl.ANY), pl.BlockSpec(memory_space=pl.ANY)),
        scratch_shapes=[
            pltpu.SemaphoreType.DMA((1,)),
            pltpu.SemaphoreType.DMA((CHUNKS,)),
            pltpu.SemaphoreType.DMA((CHUNKS,)),
            pltpu.SemaphoreType.DMA((2, n - 1)),
            pltpu.SemaphoreType.DMA((2, n - 1)),
            pltpu.SemaphoreType.DMA((CHUNKS, 6, 4)),
            pltpu.SemaphoreType.DMA((CHUNKS, 6, 4)),
            pltpu.SemaphoreType.DMA((CHUNKS, n_far // 2)),
            pltpu.SemaphoreType.DMA((CHUNKS, n_far // 2)),
        ],
        compiler_params=pltpu.CompilerParams(collective_id=0, has_side_effects=True),
    )(own_x, far_x)


def split(x):
    hi = x.astype(jnp.bfloat16)
    lo = (x - hi.astype(jnp.float32)).astype(jnp.bfloat16)
    return hi, lo


def dot_t(a, b):
    return lax.dot_general(a, b, (((1,), (1,)), ((), ())), preferred_element_type=jnp.float32)


def normal_kernel(slots, far_per, n_groups, own_meta, far_meta, own_ref, far_ref, out_ref, dense, p_hi, p_lo, x_hi, x_lo, z_hi, z_lo):
    g = pl.program_id(0)

    @pl.when(g == 0)
    def _():
        out_ref[...] = jnp.zeros_like(out_ref)

    dense[...] = jnp.zeros_like(dense)
    own_count = own_meta[(g * 3 + 2) * slots]
    for k in range(slots):

        @pl.when(k < own_count)
        def _():
            r = own_meta[(g * 3 + 0) * slots + k]
            c = own_meta[(g * 3 + 1) * slots + k]
            rows = pl.ds(pl.multiple_of(r * TB, TB), TB)
            cols = pl.ds(pl.multiple_of(c * TB, TB), TB)
            tile = own_ref[0, k * TB : (k + 1) * TB, :]
            dense[rows, cols] += tile * own_ref[0, pl.ds(slots * TB + META + c, 1), :]

    hi, lo = split(dense[...])
    p_hi[...] = hi
    p_lo[...] = lo

    for qi in range(far_per):
        base = (lax.rem(g + 1, n_groups) * far_per + qi) * 3 * slots
        count = far_meta[base + 2 * slots]
        for k in range(slots):
            r = far_meta[base + k]
            c = jnp.minimum(jnp.maximum(far_meta[base + slots + k], 0), CB_DEV - 1)
            src = pl.ds(pl.multiple_of(c * TB, TB), TB)
            x_hi[:, k * TB : (k + 1) * TB] = p_hi[:, src]
            x_lo[:, k * TB : (k + 1) * TB] = p_lo[:, src]
            t_hi, t_lo = split(far_ref[qi, k * TB : (k + 1) * TB, :])
            live = k < count
            for half in range(RB):
                keep = jnp.logical_and(live, r == half)
                z_hi[half * TB : (half + 1) * TB, k * TB : (k + 1) * TB] = jnp.where(keep, t_hi, jnp.zeros_like(t_hi))
                z_lo[half * TB : (half + 1) * TB, k * TB : (k + 1) * TB] = jnp.where(keep, t_lo, jnp.zeros_like(t_lo))
        a_hi = x_hi[...]
        b_hi = z_hi[...]
        prod = dot_t(a_hi, b_hi) + (dot_t(a_hi, z_lo[...]) + dot_t(x_lo[...], b_hi))
        out_ref[:, qi * RB * TB : (qi + 1) * RB * TB] += prod


def per_device(tiles, tile_rows, tile_cols, counts, scaling):
    n_rows = lax.axis_size("rows")
    n_cols = lax.axis_size("cols")
    slots = tiles.shape[1]
    far_per = n_rows // n_cols
    packed = pack(tiles, tile_rows, tile_cols, counts)
    set_len = packed.shape[0]
    own_packed = pack(tiles, tile_rows, tile_cols, counts, scaling)
    own_len = own_packed.shape[0]

    own, far = gather_all(own_packed, packed, n_cols, n_rows)

    own_meta = unpack_meta(own, slots)
    far_meta = unpack_meta(far, slots)
    out_cols = far_per * RB * TB

    grid_spec = pltpu.PrefetchScalarGridSpec(
        num_scalar_prefetch=2,
        grid=(n_cols,),
        in_specs=[
            pl.BlockSpec((1, own_len, TB), lambda g, om, fm: (g, 0, 0)),
            pl.BlockSpec((far_per, set_len, TB), lambda g, om, fm: ((g + 1) % n_cols, 0, 0)),
        ],
        out_specs=pl.BlockSpec((RB * TB, out_cols), lambda g, om, fm: (0, 0)),
        scratch_shapes=[
            pltpu.VMEM((RB * TB, CB_DEV * TB), jnp.float32),
            pltpu.VMEM((RB * TB, CB_DEV * TB), jnp.bfloat16),
            pltpu.VMEM((RB * TB, CB_DEV * TB), jnp.bfloat16),
            pltpu.VMEM((RB * TB, slots * TB), jnp.bfloat16),
            pltpu.VMEM((RB * TB, slots * TB), jnp.bfloat16),
            pltpu.VMEM((RB * TB, slots * TB), jnp.bfloat16),
            pltpu.VMEM((RB * TB, slots * TB), jnp.bfloat16),
        ],
    )
    return pl.pallas_call(
        functools.partial(normal_kernel, slots, far_per, n_cols),
        grid_spec=grid_spec,
        out_shape=jax.ShapeDtypeStruct((RB * TB, out_cols), jnp.float32),
        compiler_params=pltpu.CompilerParams(dimension_semantics=("arbitrary",)),
    )(own_meta, far_meta, own, far)


def solution(mesh):
    placed = (
        P("rows", "cols", None, None),
        P("rows", "cols"),
        P("rows", "cols"),
        P("rows", "cols"),
        P("cols"),
    )
    return jax.shard_map(
        per_device, mesh=mesh, in_specs=placed, out_specs=P("rows", "cols"), check_vma=False
    )
```

```python
import functools

import jax
import jax.numpy as jnp
from jax import lax
from jax.experimental import pallas as pl
from jax.experimental.pallas import tpu as pltpu
from jax.sharding import PartitionSpec as P

TB = 128
RB = 2
CB_DEV = 16
META = 8
MESH = pl.DeviceIdType.MESH
CHUNKS = 3


def pack(tiles, tile_rows, tile_cols, counts, scaling=None):
    slots = tiles.shape[1]
    meta = jnp.stack(
        [tile_rows[0], tile_cols[0], jnp.broadcast_to(counts[0, 0], (slots,))]
    ).astype(jnp.float32)
    meta = jnp.pad(meta, ((0, META - 3), (0, TB - slots)))
    parts = [tiles[0].reshape(slots * TB, TB), meta]
    if scaling is not None:
        parts += [scaling.reshape(CB_DEV, TB), jnp.zeros((META, TB), jnp.float32)]
    return jnp.concatenate(parts, axis=0)


def unpack_meta(sets, slots):
    return sets[:, slots * TB : slots * TB + 3, :slots].astype(jnp.int32).reshape(-1)


def comm_kernel(n, side, own_half, n_chunks, own_x, far_x, own_out, far_out, sems, perm_send, perm_recv, z_send, z_recv, f_send, f_recv, p_send, p_recv):
    me = lax.axis_index("cols")
    row = lax.axis_index("rows")
    core = row % 2
    y = row // (2 * side)
    x = (row // 2) % side
    step_a = (core, 1 - core)
    step_b = (1 - core, core)

    def spot(da, db, cc):
        yy = (y + da * step_a[0] + db * step_b[0] + 2 * side) % side
        xx = (x + da * step_a[1] + db * step_b[1] + 2 * side) % side
        return (yy * side + xx) * 2 + cc

    z_right = lax.rem(me + 1, n)
    z_left = lax.rem(me + n - 1, n)
    partner = row - core + (1 - core)
    far_per = far_out.shape[0] // n
    dest = (lax.rem(me + 1, n) * far_per + row % far_per, row // far_per)
    origin_plane = lax.rem(row // far_per + n - 1, n)
    source = (me * far_per + row % far_per, origin_plane)
    barrier = pltpu.get_barrier_semaphore()
    peers = [(row, z_left), (row, z_right), (partner, me), dest, source]
    for s in (1, -1):
        peers.append((spot(s, 0, core), me))
        peers.append((spot(0, s, core), me))
    for peer in peers:
        pl.semaphore_signal(barrier, inc=1, device_id=peer, device_id_type=MESH)
    pl.semaphore_wait(barrier, len(peers))

    local_own = pltpu.make_async_copy(own_x, own_out.at[me], sems.at[0])
    local_own.start()

    far_rows = far_x.shape[0]
    size = (far_rows // n_chunks) // META * META
    bounds = [h * size for h in range(n_chunks)] + [far_rows]
    chunks = []
    halves = []
    for h in range(n_chunks):
        low, high = bounds[h], bounds[h + 1]
        mid = low + ((high - low) // 2) // META * META
        chunks.append(pl.ds(low, high - low))
        halves.append((pl.ds(low, mid - low), pl.ds(mid, high - mid)))
    started = []
    partner_count = [0] * n_chunks
    partner_copies = []

    def send(src, dst, sem_s, sem_r, peer):
        copy = pltpu.make_async_remote_copy(
            src_ref=src, dst_ref=dst, send_sem=sem_s, recv_sem=sem_r, device_id=peer, device_id_type=MESH
        )
        copy.start()
        started.append(copy)
        return copy

    def to_partner(h, slot):
        j = partner_count[h]
        partner_count[h] += 1
        ref = far_out.at[slot, chunks[h]]
        partner_copies.append(send(ref, ref, p_send.at[h, j], p_recv.at[h, j], (partner, me)))

    own_halves = (pl.ds(0, own_half), pl.ds(own_half, own_half))
    z_prev = [None, None]

    def z_step(step):
        if step >= n - 1:
            return
        for way in range(2):
            if way == 0:
                origin = lax.rem(me - step + n, n)
            else:
                origin = lax.rem(me + step, n)
            if step == 0:
                src = own_x.at[own_halves[way]]
            else:
                z_prev[way].wait_recv()
                src = own_out.at[origin, own_halves[way]]
            z_prev[way] = send(
                src, own_out.at[origin, own_halves[way]], z_send.at[way, step], z_recv.at[way, step],
                (row, (z_right, z_left)[way]),
            )

    held = (0, -1, 1, 2)

    def far_stages(h):
        box = {}
        rows = chunks[h]

        def s0():
            box["moved"] = send(far_x.at[rows], far_out.at[dest[0], rows], perm_send.at[h], perm_recv.at[h], dest)

        def s1():
            box["moved"].wait_recv()
            to_partner(h, spot(0, 0, core))
            box["first"] = [
                send(far_out.at[spot(0, 0, core), rows], far_out.at[spot(0, 0, core), rows],
                     f_send.at[h, 0, w], f_recv.at[h, 0, w], (spot(s, 0, core), me))
                for w, s in enumerate((1, -1))
            ]

        def s2():
            for copy in box["first"]:
                copy.wait_recv()
            to_partner(h, spot(-1, 0, core))
            to_partner(h, spot(1, 0, core))
            box["second"] = [
                send(far_out.at[spot(-s, 0, core), halves[h][w]], far_out.at[spot(-s, 0, core), halves[h][w]],
                     f_send.at[h, 1, w], f_recv.at[h, 1, w], (spot(s, 0, core), me))
                for w, s in enumerate((1, -1))
            ]

        def s3():
            for copy in box["second"]:
                copy.wait_recv()
            to_partner(h, spot(2, 0, core))
            box["third"] = []
            for w, s in enumerate((1, -1)):
                for i, da in enumerate(held):
                    slot = spot(da, 0, core)
                    box["third"].append(send(far_out.at[slot, rows], far_out.at[slot, rows],
                                             f_send.at[h, 2 + w, i], f_recv.at[h, 2 + w, i], (spot(0, s, core), me)))

        def s4():
            for copy in box["third"]:
                copy.wait_recv()
            for s in (1, -1):
                for da in held:
                    to_partner(h, spot(da, -s, core))
            box["fourth"] = []
            for w, s in enumerate((1, -1)):
                for i, da in enumerate(held):
                    slot = spot(da, -s, core)
                    box["fourth"].append(send(far_out.at[slot, halves[h][w]], far_out.at[slot, halves[h][w]],
                                              f_send.at[h, 4 + w, i], f_recv.at[h, 4 + w, i], (spot(0, s, core), me)))

        def s5():
            for copy in box["fourth"]:
                copy.wait_recv()
            for da in held:
                to_partner(h, spot(da, 2, core))

        return [s0, s1, s2, s3, s4, s5]

    streams = [far_stages(h) for h in range(n_chunks)]
    depth = len(streams[0])
    ticks = depth + n_chunks - 1
    for tick in range(ticks):
        for h in range(n_chunks):
            if 0 <= tick - h < depth:
                streams[h][tick - h]()
        z_step(tick)
    for step in range(ticks, n - 1):
        z_step(step)
    for way in range(2):
        z_prev[way].wait_recv()
    for copy in partner_copies:
        copy.wait_recv()
    for copy in started:
        copy.wait_send()
    local_own.wait()


def gather_all(own_x, far_x, n, n_far):
    side = 4
    return pl.pallas_call(
        functools.partial(comm_kernel, n, side, own_x.shape[0] // 2, CHUNKS),
        out_shape=(
            jax.ShapeDtypeStruct((n,) + own_x.shape, own_x.dtype),
            jax.ShapeDtypeStruct((n_far,) + far_x.shape, far_x.dtype),
        ),
        in_specs=[pl.BlockSpec(memory_space=pl.ANY)] * 2,
        out_specs=(pl.BlockSpec(memory_space=pl.ANY), pl.BlockSpec(memory_space=pl.ANY)),
        scratch_shapes=[
            pltpu.SemaphoreType.DMA((1,)),
            pltpu.SemaphoreType.DMA((CHUNKS,)),
            pltpu.SemaphoreType.DMA((CHUNKS,)),
            pltpu.SemaphoreType.DMA((2, n - 1)),
            pltpu.SemaphoreType.DMA((2, n - 1)),
            pltpu.SemaphoreType.DMA((CHUNKS, 6, 4)),
            pltpu.SemaphoreType.DMA((CHUNKS, 6, 4)),
            pltpu.SemaphoreType.DMA((CHUNKS, n_far // 2)),
            pltpu.SemaphoreType.DMA((CHUNKS, n_far // 2)),
        ],
        compiler_params=pltpu.CompilerParams(collective_id=0, has_side_effects=True),
    )(own_x, far_x)


def split(x):
    hi = x.astype(jnp.bfloat16)
    lo = (x - hi.astype(jnp.float32)).astype(jnp.bfloat16)
    return hi, lo


def dot_t(a, b):
    return lax.dot_general(a, b, (((1,), (1,)), ((), ())), preferred_element_type=jnp.float32)


def normal_kernel(slots, far_per, n_groups, own_meta, far_meta, own_ref, far_ref, out_ref, dense, p_hi, p_lo, x_hi, x_lo, z_hi, z_lo):
    g = pl.program_id(0)

    @pl.when(g == 0)
    def _():
        out_ref[...] = jnp.zeros_like(out_ref)

    dense[...] = jnp.zeros_like(dense)
    own_count = own_meta[(g * 3 + 2) * slots]
    for k in range(slots):

        @pl.when(k < own_count)
        def _():
            r = own_meta[(g * 3 + 0) * slots + k]
            c = own_meta[(g * 3 + 1) * slots + k]
            rows = pl.ds(pl.multiple_of(r * TB, TB), TB)
            cols = pl.ds(pl.multiple_of(c * TB, TB), TB)
            tile = own_ref[0, k * TB : (k + 1) * TB, :]
            dense[rows, cols] += tile * own_ref[0, pl.ds(slots * TB + META + c, 1), :]

    hi, lo = split(dense[...])
    p_hi[...] = hi
    p_lo[...] = lo

    for qi in range(far_per):
        base = (lax.rem(g + 1, n_groups) * far_per + qi) * 3 * slots
        count = far_meta[base + 2 * slots]
        for k in range(slots):
            r = far_meta[base + k]
            c = jnp.minimum(jnp.maximum(far_meta[base + slots + k], 0), CB_DEV - 1)
            src = pl.ds(pl.multiple_of(c * TB, TB), TB)
            x_hi[:, k * TB : (k + 1) * TB] = p_hi[:, src]
            x_lo[:, k * TB : (k + 1) * TB] = p_lo[:, src]
            t_hi, t_lo = split(far_ref[qi, k * TB : (k + 1) * TB, :])
            live = k < count
            for half in range(RB):
                keep = jnp.logical_and(live, r == half)
                z_hi[half * TB : (half + 1) * TB, k * TB : (k + 1) * TB] = jnp.where(keep, t_hi, jnp.zeros_like(t_hi))
                z_lo[half * TB : (half + 1) * TB, k * TB : (k + 1) * TB] = jnp.where(keep, t_lo, jnp.zeros_like(t_lo))
        a_hi = x_hi[...]
        b_hi = z_hi[...]
        prod = dot_t(a_hi, b_hi) + (dot_t(a_hi, z_lo[...]) + dot_t(x_lo[...], b_hi))
        out_ref[:, qi * RB * TB : (qi + 1) * RB * TB] += prod


def per_device(tiles, tile_rows, tile_cols, counts, scaling):
    n_rows = lax.axis_size("rows")
    n_cols = lax.axis_size("cols")
    slots = tiles.shape[1]
    far_per = n_rows // n_cols
    packed = pack(tiles, tile_rows, tile_cols, counts)
    set_len = packed.shape[0]
    own_packed = pack(tiles, tile_rows, tile_cols, counts, scaling)
    own_len = own_packed.shape[0]

    own, far = gather_all(own_packed, packed, n_cols, n_rows)

    own_meta = unpack_meta(own, slots)
    far_meta = unpack_meta(far, slots)
    out_cols = far_per * RB * TB

    grid_spec = pltpu.PrefetchScalarGridSpec(
        num_scalar_prefetch=2,
        grid=(n_cols,),
        in_specs=[
            pl.BlockSpec((1, own_len, TB), lambda g, om, fm: (g, 0, 0)),
            pl.BlockSpec((far_per, set_len, TB), lambda g, om, fm: ((g + 1) % n_cols, 0, 0)),
        ],
        out_specs=pl.BlockSpec((RB * TB, out_cols), lambda g, om, fm: (0, 0)),
        scratch_shapes=[
            pltpu.VMEM((RB * TB, CB_DEV * TB), jnp.float32),
            pltpu.VMEM((RB * TB, CB_DEV * TB), jnp.bfloat16),
            pltpu.VMEM((RB * TB, CB_DEV * TB), jnp.bfloat16),
            pltpu.VMEM((RB * TB, slots * TB), jnp.bfloat16),
            pltpu.VMEM((RB * TB, slots * TB), jnp.bfloat16),
            pltpu.VMEM((RB * TB, slots * TB), jnp.bfloat16),
            pltpu.VMEM((RB * TB, slots * TB), jnp.bfloat16),
        ],
    )
    return pl.pallas_call(
        functools.partial(normal_kernel, slots, far_per, n_cols),
        grid_spec=grid_spec,
        out_shape=jax.ShapeDtypeStruct((RB * TB, out_cols), jnp.float32),
        compiler_params=pltpu.CompilerParams(dimension_semantics=("arbitrary",)),
    )(own_meta, far_meta, own, far)


def solution(mesh):
    placed = (
        P("rows", "cols", None, None),
        P("rows", "cols"),
        P("rows", "cols"),
        P("rows", "cols"),
        P("cols"),
    )
    return jax.shard_map(
        per_device, mesh=mesh, in_specs=placed, out_specs=P("rows", "cols"), check_vma=False
    )
```

```python
import functools

import jax
import jax.numpy as jnp
from jax import lax
from jax.experimental import pallas as pl
from jax.experimental.pallas import tpu as pltpu
from jax.sharding import PartitionSpec as P

TB = 128
RB = 2
CB_DEV = 16
META = 8
MESH = pl.DeviceIdType.MESH
CHUNKS = 3


def pack(tiles, tile_rows, tile_cols, counts, scaling=None):
    slots = tiles.shape[1]
    meta = jnp.stack(
        [tile_rows[0], tile_cols[0], jnp.broadcast_to(counts[0, 0], (slots,))]
    ).astype(jnp.float32)
    meta = jnp.pad(meta, ((0, META - 3), (0, TB - slots)))
    parts = [tiles[0].reshape(slots * TB, TB), meta]
    if scaling is not None:
        parts += [scaling.reshape(CB_DEV, TB), jnp.zeros((META, TB), jnp.float32)]
    return jnp.concatenate(parts, axis=0)


def unpack_meta(sets, slots):
    return sets[:, slots * TB : slots * TB + 3, :slots].astype(jnp.int32).reshape(-1)


def comm_kernel(n, side, own_half, n_chunks, own_x, far_x, own_out, far_out, sems, perm_send, perm_recv, z_send, z_recv, f_send, f_recv, p_send, p_recv):
    me = lax.axis_index("cols")
    row = lax.axis_index("rows")
    core = row % 2
    y = row // (2 * side)
    x = (row // 2) % side
    step_a = (core, 1 - core)
    step_b = (1 - core, core)

    def spot(da, db, cc):
        yy = (y + da * step_a[0] + db * step_b[0] + 2 * side) % side
        xx = (x + da * step_a[1] + db * step_b[1] + 2 * side) % side
        return (yy * side + xx) * 2 + cc

    z_right = lax.rem(me + 1, n)
    z_left = lax.rem(me + n - 1, n)
    partner = row - core + (1 - core)
    far_per = far_out.shape[0] // n
    dest = (lax.rem(me + 1, n) * far_per + row % far_per, row // far_per)
    origin_plane = lax.rem(row // far_per + n - 1, n)
    source = (me * far_per + row % far_per, origin_plane)
    barrier = pltpu.get_barrier_semaphore()
    peers = [(row, z_left), (row, z_right), (partner, me), dest, source]
    for s in (1, -1):
        peers.append((spot(s, 0, core), me))
        peers.append((spot(0, s, core), me))
    for peer in peers:
        pl.semaphore_signal(barrier, inc=1, device_id=peer, device_id_type=MESH)
    pl.semaphore_wait(barrier, len(peers))

    local_own = pltpu.make_async_copy(own_x, own_out.at[me], sems.at[0])
    local_own.start()

    far_rows = far_x.shape[0]
    size = (far_rows // n_chunks) // META * META
    bounds = [h * size for h in range(n_chunks)] + [far_rows]
    chunks = []
    halves = []
    for h in range(n_chunks):
        low, high = bounds[h], bounds[h + 1]
        mid = low + ((high - low) // 2) // META * META
        chunks.append(pl.ds(low, high - low))
        halves.append((pl.ds(low, mid - low), pl.ds(mid, high - mid)))
    started = []
    partner_count = [0] * n_chunks
    partner_copies = []

    def send(src, dst, sem_s, sem_r, peer):
        copy = pltpu.make_async_remote_copy(
            src_ref=src, dst_ref=dst, send_sem=sem_s, recv_sem=sem_r, device_id=peer, device_id_type=MESH
        )
        copy.start()
        started.append(copy)
        return copy

    def to_partner(h, slot):
        j = partner_count[h]
        partner_count[h] += 1
        ref = far_out.at[slot, chunks[h]]
        partner_copies.append(send(ref, ref, p_send.at[h, j], p_recv.at[h, j], (partner, me)))

    own_halves = (pl.ds(0, own_half), pl.ds(own_half, own_half))
    z_prev = [None, None]

    def z_step(step):
        if step >= n - 1:
            return
        for way in range(2):
            if way == 0:
                origin = lax.rem(me - step + n, n)
            else:
                origin = lax.rem(me + step, n)
            if step == 0:
                src = own_x.at[own_halves[way]]
            else:
                z_prev[way].wait_recv()
                src = own_out.at[origin, own_halves[way]]
            z_prev[way] = send(
                src, own_out.at[origin, own_halves[way]], z_send.at[way, step], z_recv.at[way, step],
                (row, (z_right, z_left)[way]),
            )

    held = (0, -1, 1, 2)

    def far_stages(h):
        box = {}
        rows = chunks[h]

        def s0():
            box["moved"] = send(far_x.at[rows], far_out.at[dest[0], rows], perm_send.at[h], perm_recv.at[h], dest)

        def s1():
            box["moved"].wait_recv()
            to_partner(h, spot(0, 0, core))
            box["first"] = [
                send(far_out.at[spot(0, 0, core), rows], far_out.at[spot(0, 0, core), rows],
                     f_send.at[h, 0, w], f_recv.at[h, 0, w], (spot(s, 0, core), me))
                for w, s in enumerate((1, -1))
            ]

        def s2():
            for copy in box["first"]:
                copy.wait_recv()
            to_partner(h, spot(-1, 0, core))
            to_partner(h, spot(1, 0, core))
            box["second"] = [
                send(far_out.at[spot(-s, 0, core), halves[h][w]], far_out.at[spot(-s, 0, core), halves[h][w]],
                     f_send.at[h, 1, w], f_recv.at[h, 1, w], (spot(s, 0, core), me))
                for w, s in enumerate((1, -1))
            ]

        def s3():
            for copy in box["second"]:
                copy.wait_recv()
            to_partner(h, spot(2, 0, core))
            box["third"] = []
            for w, s in enumerate((1, -1)):
                for i, da in enumerate(held):
                    slot = spot(da, 0, core)
                    box["third"].append(send(far_out.at[slot, rows], far_out.at[slot, rows],
                                             f_send.at[h, 2 + w, i], f_recv.at[h, 2 + w, i], (spot(0, s, core), me)))

        def s4():
            for copy in box["third"]:
                copy.wait_recv()
            for s in (1, -1):
                for da in held:
                    to_partner(h, spot(da, -s, core))
            box["fourth"] = []
            for w, s in enumerate((1, -1)):
                for i, da in enumerate(held):
                    slot = spot(da, -s, core)
                    box["fourth"].append(send(far_out.at[slot, halves[h][w]], far_out.at[slot, halves[h][w]],
                                              f_send.at[h, 4 + w, i], f_recv.at[h, 4 + w, i], (spot(0, s, core), me)))

        def s5():
            for copy in box["fourth"]:
                copy.wait_recv()
            for da in held:
                to_partner(h, spot(da, 2, core))

        return [s0, s1, s2, s3, s4, s5]

    streams = [far_stages(h) for h in range(n_chunks)]
    depth = len(streams[0])
    ticks = depth + n_chunks - 1
    for tick in range(ticks):
        z_step(tick)
        for h in range(n_chunks):
            if 0 <= tick - h < depth:
                streams[h][tick - h]()
    for step in range(ticks, n - 1):
        z_step(step)
    for way in range(2):
        z_prev[way].wait_recv()
    for copy in partner_copies:
        copy.wait_recv()
    for copy in started:
        copy.wait_send()
    local_own.wait()


def gather_all(own_x, far_x, n, n_far):
    side = 4
    return pl.pallas_call(
        functools.partial(comm_kernel, n, side, own_x.shape[0] // 2, CHUNKS),
        out_shape=(
            jax.ShapeDtypeStruct((n,) + own_x.shape, own_x.dtype),
            jax.ShapeDtypeStruct((n_far,) + far_x.shape, far_x.dtype),
        ),
        in_specs=[pl.BlockSpec(memory_space=pl.ANY)] * 2,
        out_specs=(pl.BlockSpec(memory_space=pl.ANY), pl.BlockSpec(memory_space=pl.ANY)),
        scratch_shapes=[
            pltpu.SemaphoreType.DMA((1,)),
            pltpu.SemaphoreType.DMA((CHUNKS,)),
            pltpu.SemaphoreType.DMA((CHUNKS,)),
            pltpu.SemaphoreType.DMA((2, n - 1)),
            pltpu.SemaphoreType.DMA((2, n - 1)),
            pltpu.SemaphoreType.DMA((CHUNKS, 6, 4)),
            pltpu.SemaphoreType.DMA((CHUNKS, 6, 4)),
            pltpu.SemaphoreType.DMA((CHUNKS, n_far // 2)),
            pltpu.SemaphoreType.DMA((CHUNKS, n_far // 2)),
        ],
        compiler_params=pltpu.CompilerParams(collective_id=0, has_side_effects=True),
    )(own_x, far_x)


def split(x):
    hi = x.astype(jnp.bfloat16)
    lo = (x - hi.astype(jnp.float32)).astype(jnp.bfloat16)
    return hi, lo


def dot_t(a, b):
    return lax.dot_general(a, b, (((1,), (1,)), ((), ())), preferred_element_type=jnp.float32)


def normal_kernel(slots, far_per, n_groups, own_meta, far_meta, own_ref, far_ref, out_ref, dense, p_hi, p_lo, x_hi, x_lo, z_hi, z_lo):
    g = pl.program_id(0)

    @pl.when(g == 0)
    def _():
        out_ref[...] = jnp.zeros_like(out_ref)

    dense[...] = jnp.zeros_like(dense)
    own_count = own_meta[(g * 3 + 2) * slots]
    for k in range(slots):

        @pl.when(k < own_count)
        def _():
            r = own_meta[(g * 3 + 0) * slots + k]
            c = own_meta[(g * 3 + 1) * slots + k]
            rows = pl.ds(pl.multiple_of(r * TB, TB), TB)
            cols = pl.ds(pl.multiple_of(c * TB, TB), TB)
            tile = own_ref[0, k * TB : (k + 1) * TB, :]
            dense[rows, cols] += tile * own_ref[0, pl.ds(slots * TB + META + c, 1), :]

    hi, lo = split(dense[...])
    p_hi[...] = hi
    p_lo[...] = lo

    for qi in range(far_per):
        base = (lax.rem(g + 1, n_groups) * far_per + qi) * 3 * slots
        count = far_meta[base + 2 * slots]
        for k in range(slots):
            r = far_meta[base + k]
            c = jnp.minimum(jnp.maximum(far_meta[base + slots + k], 0), CB_DEV - 1)
            src = pl.ds(pl.multiple_of(c * TB, TB), TB)
            x_hi[:, k * TB : (k + 1) * TB] = p_hi[:, src]
            x_lo[:, k * TB : (k + 1) * TB] = p_lo[:, src]
            t_hi, t_lo = split(far_ref[qi, k * TB : (k + 1) * TB, :])
            live = k < count
            for half in range(RB):
                keep = jnp.logical_and(live, r == half)
                z_hi[half * TB : (half + 1) * TB, k * TB : (k + 1) * TB] = jnp.where(keep, t_hi, jnp.zeros_like(t_hi))
                z_lo[half * TB : (half + 1) * TB, k * TB : (k + 1) * TB] = jnp.where(keep, t_lo, jnp.zeros_like(t_lo))
        a_hi = x_hi[...]
        b_hi = z_hi[...]
        prod = dot_t(a_hi, b_hi) + (dot_t(a_hi, z_lo[...]) + dot_t(x_lo[...], b_hi))
        out_ref[:, qi * RB * TB : (qi + 1) * RB * TB] += prod


def per_device(tiles, tile_rows, tile_cols, counts, scaling):
    n_rows = lax.axis_size("rows")
    n_cols = lax.axis_size("cols")
    slots = tiles.shape[1]
    far_per = n_rows // n_cols
    packed = pack(tiles, tile_rows, tile_cols, counts)
    set_len = packed.shape[0]
    own_packed = pack(tiles, tile_rows, tile_cols, counts, scaling)
    own_len = own_packed.shape[0]

    own, far = gather_all(own_packed, packed, n_cols, n_rows)

    own_meta = unpack_meta(own, slots)
    far_meta = unpack_meta(far, slots)
    out_cols = far_per * RB * TB

    grid_spec = pltpu.PrefetchScalarGridSpec(
        num_scalar_prefetch=2,
        grid=(n_cols,),
        in_specs=[
            pl.BlockSpec((1, own_len, TB), lambda g, om, fm: (g, 0, 0)),
            pl.BlockSpec((far_per, set_len, TB), lambda g, om, fm: ((g + 1) % n_cols, 0, 0)),
        ],
        out_specs=pl.BlockSpec((RB * TB, out_cols), lambda g, om, fm: (0, 0)),
        scratch_shapes=[
            pltpu.VMEM((RB * TB, CB_DEV * TB), jnp.float32),
            pltpu.VMEM((RB * TB, CB_DEV * TB), jnp.bfloat16),
            pltpu.VMEM((RB * TB, CB_DEV * TB), jnp.bfloat16),
            pltpu.VMEM((RB * TB, slots * TB), jnp.bfloat16),
            pltpu.VMEM((RB * TB, slots * TB), jnp.bfloat16),
            pltpu.VMEM((RB * TB, slots * TB), jnp.bfloat16),
            pltpu.VMEM((RB * TB, slots * TB), jnp.bfloat16),
        ],
    )
    return pl.pallas_call(
        functools.partial(normal_kernel, slots, far_per, n_cols),
        grid_spec=grid_spec,
        out_shape=jax.ShapeDtypeStruct((RB * TB, out_cols), jnp.float32),
        compiler_params=pltpu.CompilerParams(dimension_semantics=("arbitrary",)),
    )(own_meta, far_meta, own, far)


def solution(mesh):
    placed = (
        P("rows", "cols", None, None),
        P("rows", "cols"),
        P("rows", "cols"),
        P("rows", "cols"),
        P("cols"),
    )
    return jax.shard_map(
        per_device, mesh=mesh, in_specs=placed, out_specs=P("rows", "cols"), check_vma=False
    )
```

```python
import functools

import jax
import jax.numpy as jnp
from jax import lax
from jax.experimental import pallas as pl
from jax.experimental.pallas import tpu as pltpu
from jax.sharding import PartitionSpec as P

TB = 128
RB = 2
CB_DEV = 16
META = 8
MESH = pl.DeviceIdType.MESH
CHUNKS = 3


def pack(tiles, tile_rows, tile_cols, counts, scaling=None):
    slots = tiles.shape[1]
    meta = jnp.stack(
        [tile_rows[0], tile_cols[0], jnp.broadcast_to(counts[0, 0], (slots,))]
    ).astype(jnp.float32)
    meta = jnp.pad(meta, ((0, META - 3), (0, TB - slots)))
    parts = [tiles[0].reshape(slots * TB, TB), meta]
    if scaling is not None:
        parts += [scaling.reshape(CB_DEV, TB), jnp.zeros((META, TB), jnp.float32)]
    return jnp.concatenate(parts, axis=0)


def unpack_meta(sets, slots):
    return sets[:, slots * TB : slots * TB + 3, :slots].astype(jnp.int32).reshape(-1)


def comm_kernel(n, side, own_half, n_chunks, own_x, far_x, own_out, far_out, sems, perm_send, perm_recv, z_send, z_recv, f_send, f_recv, p_send, p_recv):
    me = lax.axis_index("cols")
    row = lax.axis_index("rows")
    core = row % 2
    y = row // (2 * side)
    x = (row // 2) % side
    step_a = (core, 1 - core)
    step_b = (1 - core, core)

    def spot(da, db, cc):
        yy = (y + da * step_a[0] + db * step_b[0] + 2 * side) % side
        xx = (x + da * step_a[1] + db * step_b[1] + 2 * side) % side
        return (yy * side + xx) * 2 + cc

    z_right = lax.rem(me + 1, n)
    z_left = lax.rem(me + n - 1, n)
    partner = row - core + (1 - core)
    far_per = far_out.shape[0] // n
    dest = (lax.rem(me + 1, n) * far_per + row % far_per, row // far_per)
    origin_plane = lax.rem(row // far_per + n - 1, n)
    source = (me * far_per + row % far_per, origin_plane)
    barrier = pltpu.get_barrier_semaphore()
    peers = [(row, z_left), (row, z_right), (partner, me), dest, source]
    for s in (1, -1):
        peers.append((spot(s, 0, core), me))
        peers.append((spot(0, s, core), me))
    for peer in peers:
        pl.semaphore_signal(barrier, inc=1, device_id=peer, device_id_type=MESH)
    pl.semaphore_wait(barrier, len(peers))

    local_own = pltpu.make_async_copy(own_x, own_out.at[me], sems.at[0])
    local_own.start()

    far_rows = far_x.shape[0]
    size = (far_rows // n_chunks) // META * META
    bounds = [h * size for h in range(n_chunks)] + [far_rows]
    chunks = []
    halves = []
    for h in range(n_chunks):
        low, high = bounds[h], bounds[h + 1]
        mid = low + ((high - low) // 2) // META * META
        chunks.append(pl.ds(low, high - low))
        halves.append((pl.ds(low, mid - low), pl.ds(mid, high - mid)))
    started = []
    partner_count = [0] * n_chunks
    partner_copies = []

    def send(src, dst, sem_s, sem_r, peer):
        copy = pltpu.make_async_remote_copy(
            src_ref=src, dst_ref=dst, send_sem=sem_s, recv_sem=sem_r, device_id=peer, device_id_type=MESH
        )
        copy.start()
        started.append(copy)
        return copy

    def to_partner(h, slot):
        j = partner_count[h]
        partner_count[h] += 1
        ref = far_out.at[slot, chunks[h]]
        partner_copies.append(send(ref, ref, p_send.at[h, j], p_recv.at[h, j], (partner, me)))

    own_halves = (pl.ds(0, own_half), pl.ds(own_half, own_half))
    z_prev = [None, None]

    def z_step(step):
        if step >= n - 1:
            return
        for way in range(2):
            if way == 0:
                origin = lax.rem(me - step + n, n)
            else:
                origin = lax.rem(me + step, n)
            if step == 0:
                src = own_x.at[own_halves[way]]
            else:
                z_prev[way].wait_recv()
                src = own_out.at[origin, own_halves[way]]
            z_prev[way] = send(
                src, own_out.at[origin, own_halves[way]], z_send.at[way, step], z_recv.at[way, step],
                (row, (z_right, z_left)[way]),
            )

    held = (0, -1, 1, 2)

    def far_stages(h):
        box = {}
        rows = chunks[h]

        def s0():
            box["moved"] = send(far_x.at[rows], far_out.at[dest[0], rows], perm_send.at[h], perm_recv.at[h], dest)

        def s1():
            box["moved"].wait_recv()
            to_partner(h, spot(0, 0, core))
            box["first"] = [
                send(far_out.at[spot(0, 0, core), rows], far_out.at[spot(0, 0, core), rows],
                     f_send.at[h, 0, w], f_recv.at[h, 0, w], (spot(s, 0, core), me))
                for w, s in enumerate((1, -1))
            ]

        def s2():
            for copy in box["first"]:
                copy.wait_recv()
            to_partner(h, spot(-1, 0, core))
            to_partner(h, spot(1, 0, core))
            box["second"] = [
                send(far_out.at[spot(-s, 0, core), halves[h][w]], far_out.at[spot(-s, 0, core), halves[h][w]],
                     f_send.at[h, 1, w], f_recv.at[h, 1, w], (spot(s, 0, core), me))
                for w, s in enumerate((1, -1))
            ]

        def s3():
            for copy in box["second"]:
                copy.wait_recv()
            to_partner(h, spot(2, 0, core))
            box["third"] = []
            for w, s in enumerate((1, -1)):
                for i, da in enumerate(held):
                    slot = spot(da, 0, core)
                    box["third"].append(send(far_out.at[slot, rows], far_out.at[slot, rows],
                                             f_send.at[h, 2 + w, i], f_recv.at[h, 2 + w, i], (spot(0, s, core), me)))

        def s4():
            for copy in box["third"]:
                copy.wait_recv()
            for s in (1, -1):
                for da in held:
                    to_partner(h, spot(da, -s, core))
            box["fourth"] = []
            for w, s in enumerate((1, -1)):
                for i, da in enumerate(held):
                    slot = spot(da, -s, core)
                    box["fourth"].append(send(far_out.at[slot, halves[h][w]], far_out.at[slot, halves[h][w]],
                                              f_send.at[h, 4 + w, i], f_recv.at[h, 4 + w, i], (spot(0, s, core), me)))

        def s5():
            for copy in box["fourth"]:
                copy.wait_recv()
            for da in held:
                to_partner(h, spot(da, 2, core))

        return [s0, s1, s2, s3, s4, s5]

    streams = [far_stages(h) for h in range(n_chunks)]
    depth = len(streams[0])
    ticks = depth + n_chunks - 1
    for tick in range(ticks):
        for h in range(n_chunks):
            if 0 <= tick - h < depth:
                streams[h][tick - h]()
        if tick >= 1:
            z_step(tick - 1)
    for step in range(ticks - 1, n - 1):
        z_step(step)
    for way in range(2):
        z_prev[way].wait_recv()
    for copy in partner_copies:
        copy.wait_recv()
    for copy in started:
        copy.wait_send()
    local_own.wait()


def gather_all(own_x, far_x, n, n_far):
    side = 4
    return pl.pallas_call(
        functools.partial(comm_kernel, n, side, own_x.shape[0] // 2, CHUNKS),
        out_shape=(
            jax.ShapeDtypeStruct((n,) + own_x.shape, own_x.dtype),
            jax.ShapeDtypeStruct((n_far,) + far_x.shape, far_x.dtype),
        ),
        in_specs=[pl.BlockSpec(memory_space=pl.ANY)] * 2,
        out_specs=(pl.BlockSpec(memory_space=pl.ANY), pl.BlockSpec(memory_space=pl.ANY)),
        scratch_shapes=[
            pltpu.SemaphoreType.DMA((1,)),
            pltpu.SemaphoreType.DMA((CHUNKS,)),
            pltpu.SemaphoreType.DMA((CHUNKS,)),
            pltpu.SemaphoreType.DMA((2, n - 1)),
            pltpu.SemaphoreType.DMA((2, n - 1)),
            pltpu.SemaphoreType.DMA((CHUNKS, 6, 4)),
            pltpu.SemaphoreType.DMA((CHUNKS, 6, 4)),
            pltpu.SemaphoreType.DMA((CHUNKS, n_far // 2)),
            pltpu.SemaphoreType.DMA((CHUNKS, n_far // 2)),
        ],
        compiler_params=pltpu.CompilerParams(collective_id=0, has_side_effects=True),
    )(own_x, far_x)


def split(x):
    hi = x.astype(jnp.bfloat16)
    lo = (x - hi.astype(jnp.float32)).astype(jnp.bfloat16)
    return hi, lo


def dot_t(a, b):
    return lax.dot_general(a, b, (((1,), (1,)), ((), ())), preferred_element_type=jnp.float32)


def normal_kernel(slots, far_per, n_groups, own_meta, far_meta, own_ref, far_ref, out_ref, dense, p_hi, p_lo, x_hi, x_lo, z_hi, z_lo):
    g = pl.program_id(0)

    @pl.when(g == 0)
    def _():
        out_ref[...] = jnp.zeros_like(out_ref)

    dense[...] = jnp.zeros_like(dense)
    own_count = own_meta[(g * 3 + 2) * slots]
    for k in range(slots):

        @pl.when(k < own_count)
        def _():
            r = own_meta[(g * 3 + 0) * slots + k]
            c = own_meta[(g * 3 + 1) * slots + k]
            rows = pl.ds(pl.multiple_of(r * TB, TB), TB)
            cols = pl.ds(pl.multiple_of(c * TB, TB), TB)
            tile = own_ref[0, k * TB : (k + 1) * TB, :]
            dense[rows, cols] += tile * own_ref[0, pl.ds(slots * TB + META + c, 1), :]

    hi, lo = split(dense[...])
    p_hi[...] = hi
    p_lo[...] = lo

    for qi in range(far_per):
        base = (lax.rem(g + 1, n_groups) * far_per + qi) * 3 * slots
        count = far_meta[base + 2 * slots]
        for k in range(slots):
            r = far_meta[base + k]
            c = jnp.minimum(jnp.maximum(far_meta[base + slots + k], 0), CB_DEV - 1)
            src = pl.ds(pl.multiple_of(c * TB, TB), TB)
            x_hi[:, k * TB : (k + 1) * TB] = p_hi[:, src]
            x_lo[:, k * TB : (k + 1) * TB] = p_lo[:, src]
            t_hi, t_lo = split(far_ref[qi, k * TB : (k + 1) * TB, :])
            live = k < count
            for half in range(RB):
                keep = jnp.logical_and(live, r == half)
                z_hi[half * TB : (half + 1) * TB, k * TB : (k + 1) * TB] = jnp.where(keep, t_hi, jnp.zeros_like(t_hi))
                z_lo[half * TB : (half + 1) * TB, k * TB : (k + 1) * TB] = jnp.where(keep, t_lo, jnp.zeros_like(t_lo))
        a_hi = x_hi[...]
        b_hi = z_hi[...]
        prod = dot_t(a_hi, b_hi) + (dot_t(a_hi, z_lo[...]) + dot_t(x_lo[...], b_hi))
        out_ref[:, qi * RB * TB : (qi + 1) * RB * TB] += prod


def per_device(tiles, tile_rows, tile_cols, counts, scaling):
    n_rows = lax.axis_size("rows")
    n_cols = lax.axis_size("cols")
    slots = tiles.shape[1]
    far_per = n_rows // n_cols
    packed = pack(tiles, tile_rows, tile_cols, counts)
    set_len = packed.shape[0]
    own_packed = pack(tiles, tile_rows, tile_cols, counts, scaling)
    own_len = own_packed.shape[0]

    own, far = gather_all(own_packed, packed, n_cols, n_rows)

    own_meta = unpack_meta(own, slots)
    far_meta = unpack_meta(far, slots)
    out_cols = far_per * RB * TB

    grid_spec = pltpu.PrefetchScalarGridSpec(
        num_scalar_prefetch=2,
        grid=(n_cols,),
        in_specs=[
            pl.BlockSpec((1, own_len, TB), lambda g, om, fm: (g, 0, 0)),
            pl.BlockSpec((far_per, set_len, TB), lambda g, om, fm: ((g + 1) % n_cols, 0, 0)),
        ],
        out_specs=pl.BlockSpec((RB * TB, out_cols), lambda g, om, fm: (0, 0)),
        scratch_shapes=[
            pltpu.VMEM((RB * TB, CB_DEV * TB), jnp.float32),
            pltpu.VMEM((RB * TB, CB_DEV * TB), jnp.bfloat16),
            pltpu.VMEM((RB * TB, CB_DEV * TB), jnp.bfloat16),
            pltpu.VMEM((RB * TB, slots * TB), jnp.bfloat16),
            pltpu.VMEM((RB * TB, slots * TB), jnp.bfloat16),
            pltpu.VMEM((RB * TB, slots * TB), jnp.bfloat16),
            pltpu.VMEM((RB * TB, slots * TB), jnp.bfloat16),
        ],
    )
    return pl.pallas_call(
        functools.partial(normal_kernel, slots, far_per, n_cols),
        grid_spec=grid_spec,
        out_shape=jax.ShapeDtypeStruct((RB * TB, out_cols), jnp.float32),
        compiler_params=pltpu.CompilerParams(dimension_semantics=("arbitrary",)),
    )(own_meta, far_meta, own, far)


def solution(mesh):
    placed = (
        P("rows", "cols", None, None),
        P("rows", "cols"),
        P("rows", "cols"),
        P("rows", "cols"),
        P("cols"),
    )
    return jax.shard_map(
        per_device, mesh=mesh, in_specs=placed, out_specs=P("rows", "cols"), check_vma=False
    )
```

```python
import functools

import jax
import jax.numpy as jnp
from jax import lax
from jax.experimental import pallas as pl
from jax.experimental.pallas import tpu as pltpu
from jax.sharding import PartitionSpec as P

TB = 128
RB = 2
CB_DEV = 16
META = 8
MESH = pl.DeviceIdType.MESH
CHUNKS = 5


def pack(tiles, tile_rows, tile_cols, counts, scaling=None):
    slots = tiles.shape[1]
    meta = jnp.stack(
        [tile_rows[0], tile_cols[0], jnp.broadcast_to(counts[0, 0], (slots,))]
    ).astype(jnp.float32)
    meta = jnp.pad(meta, ((0, META - 3), (0, TB - slots)))
    parts = [tiles[0].reshape(slots * TB, TB), meta]
    if scaling is not None:
        parts += [scaling.reshape(CB_DEV, TB), jnp.zeros((META, TB), jnp.float32)]
    return jnp.concatenate(parts, axis=0)


def unpack_meta(sets, slots):
    return sets[:, slots * TB : slots * TB + 3, :slots].astype(jnp.int32).reshape(-1)


def comm_kernel(n, side, own_half, n_chunks, own_x, far_x, own_out, far_out, sems, perm_send, perm_recv, z_send, z_recv, f_send, f_recv, p_send, p_recv):
    me = lax.axis_index("cols")
    row = lax.axis_index("rows")
    core = row % 2
    y = row // (2 * side)
    x = (row // 2) % side
    step_a = (core, 1 - core)
    step_b = (1 - core, core)

    def spot(da, db, cc):
        yy = (y + da * step_a[0] + db * step_b[0] + 2 * side) % side
        xx = (x + da * step_a[1] + db * step_b[1] + 2 * side) % side
        return (yy * side + xx) * 2 + cc

    z_right = lax.rem(me + 1, n)
    z_left = lax.rem(me + n - 1, n)
    partner = row - core + (1 - core)
    far_per = far_out.shape[0] // n
    dest = (lax.rem(me + 1, n) * far_per + row % far_per, row // far_per)
    origin_plane = lax.rem(row // far_per + n - 1, n)
    source = (me * far_per + row % far_per, origin_plane)
    barrier = pltpu.get_barrier_semaphore()
    peers = [(row, z_left), (row, z_right), (partner, me), dest, source]
    for s in (1, -1):
        peers.append((spot(s, 0, core), me))
        peers.append((spot(0, s, core), me))
    for peer in peers:
        pl.semaphore_signal(barrier, inc=1, device_id=peer, device_id_type=MESH)
    pl.semaphore_wait(barrier, len(peers))

    local_own = pltpu.make_async_copy(own_x, own_out.at[me], sems.at[0])
    local_own.start()

    far_rows = far_x.shape[0]
    size = (far_rows // n_chunks) // META * META
    bounds = [h * size for h in range(n_chunks)] + [far_rows]
    chunks = []
    halves = []
    for h in range(n_chunks):
        low, high = bounds[h], bounds[h + 1]
        mid = low + ((high - low) // 2) // META * META
        chunks.append(pl.ds(low, high - low))
        halves.append((pl.ds(low, mid - low), pl.ds(mid, high - mid)))
    started = []
    partner_count = [0] * n_chunks
    partner_copies = []

    def send(src, dst, sem_s, sem_r, peer):
        copy = pltpu.make_async_remote_copy(
            src_ref=src, dst_ref=dst, send_sem=sem_s, recv_sem=sem_r, device_id=peer, device_id_type=MESH
        )
        copy.start()
        started.append(copy)
        return copy

    def to_partner(h, slot):
        j = partner_count[h]
        partner_count[h] += 1
        ref = far_out.at[slot, chunks[h]]
        partner_copies.append(send(ref, ref, p_send.at[h, j], p_recv.at[h, j], (partner, me)))

    own_halves = (pl.ds(0, own_half), pl.ds(own_half, own_half))
    z_prev = [None, None]

    def z_step(step):
        if step >= n - 1:
            return
        for way in range(2):
            if way == 0:
                origin = lax.rem(me - step + n, n)
            else:
                origin = lax.rem(me + step, n)
            if step == 0:
                src = own_x.at[own_halves[way]]
            else:
                z_prev[way].wait_recv()
                src = own_out.at[origin, own_halves[way]]
            z_prev[way] = send(
                src, own_out.at[origin, own_halves[way]], z_send.at[way, step], z_recv.at[way, step],
                (row, (z_right, z_left)[way]),
            )

    held = (0, -1, 1, 2)

    def far_stages(h):
        box = {}
        rows = chunks[h]

        def s0():
            box["moved"] = send(far_x.at[rows], far_out.at[dest[0], rows], perm_send.at[h], perm_recv.at[h], dest)

        def s1():
            box["moved"].wait_recv()
            to_partner(h, spot(0, 0, core))
            box["first"] = [
                send(far_out.at[spot(0, 0, core), rows], far_out.at[spot(0, 0, core), rows],
                     f_send.at[h, 0, w], f_recv.at[h, 0, w], (spot(s, 0, core), me))
                for w, s in enumerate((1, -1))
            ]

        def s2():
            for copy in box["first"]:
                copy.wait_recv()
            to_partner(h, spot(-1, 0, core))
            to_partner(h, spot(1, 0, core))
            box["second"] = [
                send(far_out.at[spot(-s, 0, core), halves[h][w]], far_out.at[spot(-s, 0, core), halves[h][w]],
                     f_send.at[h, 1, w], f_recv.at[h, 1, w], (spot(s, 0, core), me))
                for w, s in enumerate((1, -1))
            ]

        def s3():
            for copy in box["second"]:
                copy.wait_recv()
            to_partner(h, spot(2, 0, core))
            box["third"] = []
            for w, s in enumerate((1, -1)):
                for i, da in enumerate(held):
                    slot = spot(da, 0, core)
                    box["third"].append(send(far_out.at[slot, rows], far_out.at[slot, rows],
                                             f_send.at[h, 2 + w, i], f_recv.at[h, 2 + w, i], (spot(0, s, core), me)))

        def s4():
            for copy in box["third"]:
                copy.wait_recv()
            for s in (1, -1):
                for da in held:
                    to_partner(h, spot(da, -s, core))
            box["fourth"] = []
            for w, s in enumerate((1, -1)):
                for i, da in enumerate(held):
                    slot = spot(da, -s, core)
                    box["fourth"].append(send(far_out.at[slot, halves[h][w]], far_out.at[slot, halves[h][w]],
                                              f_send.at[h, 4 + w, i], f_recv.at[h, 4 + w, i], (spot(0, s, core), me)))

        def s5():
            for copy in box["fourth"]:
                copy.wait_recv()
            for da in held:
                to_partner(h, spot(da, 2, core))

        return [s0, s1, s2, s3, s4, s5]

    streams = [far_stages(h) for h in range(n_chunks)]
    depth = len(streams[0])
    ticks = depth + n_chunks - 1
    for tick in range(ticks):
        for h in range(n_chunks):
            if 0 <= tick - h < depth:
                streams[h][tick - h]()
        z_step(tick)
    for step in range(ticks, n - 1):
        z_step(step)
    for way in range(2):
        z_prev[way].wait_recv()
    for copy in partner_copies:
        copy.wait_recv()
    for copy in started:
        copy.wait_send()
    local_own.wait()


def gather_all(own_x, far_x, n, n_far):
    side = 4
    return pl.pallas_call(
        functools.partial(comm_kernel, n, side, own_x.shape[0] // 2, CHUNKS),
        out_shape=(
            jax.ShapeDtypeStruct((n,) + own_x.shape, own_x.dtype),
            jax.ShapeDtypeStruct((n_far,) + far_x.shape, far_x.dtype),
        ),
        in_specs=[pl.BlockSpec(memory_space=pl.ANY)] * 2,
        out_specs=(pl.BlockSpec(memory_space=pl.ANY), pl.BlockSpec(memory_space=pl.ANY)),
        scratch_shapes=[
            pltpu.SemaphoreType.DMA((1,)),
            pltpu.SemaphoreType.DMA((CHUNKS,)),
            pltpu.SemaphoreType.DMA((CHUNKS,)),
            pltpu.SemaphoreType.DMA((2, n - 1)),
            pltpu.SemaphoreType.DMA((2, n - 1)),
            pltpu.SemaphoreType.DMA((CHUNKS, 6, 4)),
            pltpu.SemaphoreType.DMA((CHUNKS, 6, 4)),
            pltpu.SemaphoreType.DMA((CHUNKS, n_far // 2)),
            pltpu.SemaphoreType.DMA((CHUNKS, n_far // 2)),
        ],
        compiler_params=pltpu.CompilerParams(collective_id=0, has_side_effects=True),
    )(own_x, far_x)


def split(x):
    hi = x.astype(jnp.bfloat16)
    lo = (x - hi.astype(jnp.float32)).astype(jnp.bfloat16)
    return hi, lo


def dot_t(a, b):
    return lax.dot_general(a, b, (((1,), (1,)), ((), ())), preferred_element_type=jnp.float32)


def normal_kernel(slots, far_per, n_groups, own_meta, far_meta, own_ref, far_ref, out_ref, dense, p_hi, p_lo, x_hi, x_lo, z_hi, z_lo):
    g = pl.program_id(0)

    @pl.when(g == 0)
    def _():
        out_ref[...] = jnp.zeros_like(out_ref)

    dense[...] = jnp.zeros_like(dense)
    own_count = own_meta[(g * 3 + 2) * slots]
    for k in range(slots):

        @pl.when(k < own_count)
        def _():
            r = own_meta[(g * 3 + 0) * slots + k]
            c = own_meta[(g * 3 + 1) * slots + k]
            rows = pl.ds(pl.multiple_of(r * TB, TB), TB)
            cols = pl.ds(pl.multiple_of(c * TB, TB), TB)
            tile = own_ref[0, k * TB : (k + 1) * TB, :]
            dense[rows, cols] += tile * own_ref[0, pl.ds(slots * TB + META + c, 1), :]

    hi, lo = split(dense[...])
    p_hi[...] = hi
    p_lo[...] = lo

    for qi in range(far_per):
        base = (lax.rem(g + 1, n_groups) * far_per + qi) * 3 * slots
        count = far_meta[base + 2 * slots]
        for k in range(slots):
            r = far_meta[base + k]
            c = jnp.minimum(jnp.maximum(far_meta[base + slots + k], 0), CB_DEV - 1)
            src = pl.ds(pl.multiple_of(c * TB, TB), TB)
            x_hi[:, k * TB : (k + 1) * TB] = p_hi[:, src]
            x_lo[:, k * TB : (k + 1) * TB] = p_lo[:, src]
            t_hi, t_lo = split(far_ref[qi, k * TB : (k + 1) * TB, :])
            live = k < count
            for half in range(RB):
                keep = jnp.logical_and(live, r == half)
                z_hi[half * TB : (half + 1) * TB, k * TB : (k + 1) * TB] = jnp.where(keep, t_hi, jnp.zeros_like(t_hi))
                z_lo[half * TB : (half + 1) * TB, k * TB : (k + 1) * TB] = jnp.where(keep, t_lo, jnp.zeros_like(t_lo))
        a_hi = x_hi[...]
        b_hi = z_hi[...]
        prod = dot_t(a_hi, b_hi) + (dot_t(a_hi, z_lo[...]) + dot_t(x_lo[...], b_hi))
        out_ref[:, qi * RB * TB : (qi + 1) * RB * TB] += prod


def per_device(tiles, tile_rows, tile_cols, counts, scaling):
    n_rows = lax.axis_size("rows")
    n_cols = lax.axis_size("cols")
    slots = tiles.shape[1]
    far_per = n_rows // n_cols
    packed = pack(tiles, tile_rows, tile_cols, counts)
    set_len = packed.shape[0]
    own_packed = pack(tiles, tile_rows, tile_cols, counts, scaling)
    own_len = own_packed.shape[0]

    own, far = gather_all(own_packed, packed, n_cols, n_rows)

    own_meta = unpack_meta(own, slots)
    far_meta = unpack_meta(far, slots)
    out_cols = far_per * RB * TB

    grid_spec = pltpu.PrefetchScalarGridSpec(
        num_scalar_prefetch=2,
        grid=(n_cols,),
        in_specs=[
            pl.BlockSpec((1, own_len, TB), lambda g, om, fm: (g, 0, 0)),
            pl.BlockSpec((far_per, set_len, TB), lambda g, om, fm: ((g + 1) % n_cols, 0, 0)),
        ],
        out_specs=pl.BlockSpec((RB * TB, out_cols), lambda g, om, fm: (0, 0)),
        scratch_shapes=[
            pltpu.VMEM((RB * TB, CB_DEV * TB), jnp.float32),
            pltpu.VMEM((RB * TB, CB_DEV * TB), jnp.bfloat16),
            pltpu.VMEM((RB * TB, CB_DEV * TB), jnp.bfloat16),
            pltpu.VMEM((RB * TB, slots * TB), jnp.bfloat16),
            pltpu.VMEM((RB * TB, slots * TB), jnp.bfloat16),
            pltpu.VMEM((RB * TB, slots * TB), jnp.bfloat16),
            pltpu.VMEM((RB * TB, slots * TB), jnp.bfloat16),
        ],
    )
    return pl.pallas_call(
        functools.partial(normal_kernel, slots, far_per, n_cols),
        grid_spec=grid_spec,
        out_shape=jax.ShapeDtypeStruct((RB * TB, out_cols), jnp.float32),
        compiler_params=pltpu.CompilerParams(dimension_semantics=("arbitrary",)),
    )(own_meta, far_meta, own, far)


def solution(mesh):
    placed = (
        P("rows", "cols", None, None),
        P("rows", "cols"),
        P("rows", "cols"),
        P("rows", "cols"),
        P("cols"),
    )
    return jax.shard_map(
        per_device, mesh=mesh, in_specs=placed, out_specs=P("rows", "cols"), check_vma=False
    )
```
